256 devices in a mesh: tower: 2 (over x_lo), blk: 128 (over z, y, x_hi, core).
Axes of the slice: x: 4 (x_hi: 2, x_lo: 2; x = x_hi * 2 + x_lo), y: 4, z: 8, core: 2. Of those that a mesh axis runs over, the one named last changes fastest.
Arguments:
- pooled: bfloat16 [2, 16384, 1152], P('tower', 'blk'), may hold values from -6 to 6
- final_gain: float32 [2, 1152], P('tower'), may hold values from 0.5 to 1.5
- head_weight: bfloat16 [2, 1152, 1152], P('tower'), may hold values from -0.1875 to 0.1875
- pair_ids: int32 [16384], replicated, may hold values from 0 to 16383
- log_scale: float32 [1], replicated, may hold values from 4.2 to 4.7
- bias: float32 [1], replicated, may hold values from -4 to -1
Outputs:
- emb_grad: float32 [2, 16384, 1152], P('tower', 'blk')
The draws below stay inside these ranges and needn't reach their ends.
Inputs may be any that keep to these rules, and one draw needn't show every extreme that they name: `pair_ids`: examples with equal ids form positive pairs; every example is a positive pair with its own image and text.
All inputs are finite; a program needn't handle non-finite values.
Results may differ from the reference program's by a relative error of at most 0.0043.
Values may be sent and summed in bfloat16 or wider, within the bound.
A program may use at most 192 MiB of HBM per device.

```python
import jax
import jax.numpy as jnp
from jax import lax

D = 1152
EX_DEV = 128
BATCH = 16384


def set_ends(entries, rng, low, top_value):
    extent = entries.shape
    place = [jax.random.randint(jax.random.fold_in(rng, axis), (), 0, extent[axis]) for axis in range(len(extent))]
    entries = entries.at[tuple(place)].set(low)
    longest = extent.index(max(extent))
    place[longest] = (place[longest] + 1) % extent[longest]
    return entries.at[tuple(place)].set(top_value)


def levels(rng, dims, split, low, high):
    def one(dim, blocks):
        steps = jax.random.uniform(jax.random.fold_in(jax.random.fold_in(rng, 6), dim), (blocks,), jnp.float32, low / len(split), high / len(split))
        return jnp.repeat(jnp.exp(steps), dims[dim] // blocks).reshape((-1,) + (1,) * (len(dims) - dim - 1))

    level = one(*split[0])
    for cut in split[1:]:
        level = level * one(*cut)
    return level


def bell_draw(rng, dims, width, bound, pieces=(), kind=jnp.bfloat16):
    array = width * jax.random.normal(rng, dims, jnp.float32)
    if pieces:
        array = array * levels(rng, dims, pieces, -0.22, 0.18)
    return jnp.clip(array, -bound, bound).astype(kind)


def setup_inputs(seed: int = 0) -> dict:
    key_list = jax.random.split(jax.random.key(seed), 7)
    pooled = bell_draw(key_list[0], (2, BATCH, D), 1.0, 6.0, ((0, 2), (1, 128)))
    final_gain = jnp.clip(0.5 + 1.0 * jax.random.uniform(key_list[1], (2, D), jnp.float32) ** levels(key_list[1], (2, D), ((0, 2),), -0.2, 0.2), 0.5, 1.5)
    head_weight = bell_draw(key_list[2], (2, D, D), D ** -0.5, 0.1875, ((0, 2),))
    pair_ids = set_ends(jax.random.randint(key_list[3], (BATCH,), 0, BATCH), jax.random.fold_in(key_list[3], 1), 0, BATCH - 1).astype(jnp.int32)
    log_scale = jnp.clip(jax.random.uniform(key_list[4], (1,), jnp.float32, 4.2, 4.7), 4.2, 4.7)
    bias = jnp.clip(jax.random.uniform(key_list[5], (1,), jnp.float32, -4.0, -1.0), -4.0, -1.0)
    return {"pooled": pooled, "final_gain": final_gain, "head_weight": head_weight, "pair_ids": pair_ids, "log_scale": log_scale, "bias": bias}


def embed_rows(feats, gain, weight):
    values = feats.astype(jnp.float32)
    center = values - lax.optimization_barrier(jnp.mean(values, axis=-1, keepdims=True))
    spread = lax.optimization_barrier(jnp.mean(center * center, axis=-1, keepdims=True))
    normed = (center * lax.rsqrt(spread + 1e-06) * gain).astype(jnp.bfloat16)
    head = jnp.dot(normed, weight, preferred_element_type=jnp.float32)
    length = lax.optimization_barrier(jnp.sum(head * head, axis=-1, keepdims=True))
    return (head * lax.rsqrt(length + 1e-06)).astype(jnp.bfloat16)

def pair_forces(fixed_rows, moving_rows, fixed_ids, moving_ids, scale, shift):
    logits = scale * lax.dot_general(fixed_rows, moving_rows, (((1,), (1,)), ((), ())), preferred_element_type=jnp.float32) + shift
    sign = jnp.where(fixed_ids[:, None] == moving_ids[None, :], jnp.float32(1.0), jnp.float32(-1.0))
    coef = (-sign * jax.nn.sigmoid(-sign * logits)).astype(jnp.bfloat16)
    return jnp.dot(coef, moving_rows, preferred_element_type=jnp.float32)

def reference(pooled, final_gain, head_weight, pair_ids, log_scale, bias):
    images = embed_rows(pooled[0], final_gain[0], head_weight[0])
    texts = embed_rows(pooled[1], final_gain[1], head_weight[1])
    scale = jnp.exp(log_scale[0])
    shift = bias[0]
    blocks = BATCH // EX_DEV
    id_blocks = pair_ids.reshape(blocks, EX_DEV)

    def image_block(item):
        rows, ids = item
        return pair_forces(rows, texts, ids, pair_ids, scale, shift)

    def text_block(item):
        rows, ids = item
        return pair_forces(rows, images, ids, pair_ids, scale, shift)
    image_grad = lax.map(image_block, (images.reshape(blocks, EX_DEV, D), id_blocks)).reshape(BATCH, D)
    text_grad = lax.map(text_block, (texts.reshape(blocks, EX_DEV, D), id_blocks)).reshape(BATCH, D)
    return jnp.stack([image_grad, text_grad])
```

```python
import jax
import jax.numpy as jnp
from jax import lax
from jax.experimental import pallas as pl
from jax.experimental.pallas import tpu as pltpu
from jax.sharding import PartitionSpec as P

MESH = pl.DeviceIdType.MESH
BF = jnp.bfloat16
F32 = jnp.float32

Y_SLOT = {2: 0, 0: 1, 1: 2, -1: 3}
Z_SLOT = {4: 0, 3: 1, -3: 2, 2: 3, -2: 4, 1: 5, -1: 6, 0: 7}
UNITS = ((0, 384), (384, 256), (640, 384))
Z_OUT = ((0, 1), (1, 1), (0, 2), (1, 2), (0, 3), (1, 3), (0, 4))
Z_BACK = ((0, 4), (1, 3), (0, 3), (1, 2), (0, 2), (1, 1), (0, 1))


def kernel(
    pooled, gain, weight, ids, log_scale, bias, out,
    w_buf, emb, img, txt, coef, g_img, g_txt, s_img, s_x, s_txt, r_sib, r_z, r_y2, r_y1, r_x, r_fin,
    img_ids, txt_ids,
    w_sem, sx, rx, stx, rtx, sy, ry, sz, rz, ss, rs, ss2, rs2, szr, rzr, syr, ryr, sxr, rxr, sf, rf,
):
    t = lax.axis_index("tower")
    b = lax.axis_index("blk")
    c = lax.rem(b, 2)
    h = lax.rem(b // 2, 2)
    y = lax.rem(b // 4, 4)
    z = b // 16
    x = h * 2 + t
    is_img = t == 0
    is_txt = t == 1
    home = c == t
    guest = c != t

    def at(dx=0, dy=0, dz=0, dc=0):
        nx = lax.rem(x + dx + 4, 4)
        ny = lax.rem(y + dy + 4, 4)
        nz = lax.rem(z + dz + 8, 8)
        nc = lax.rem(c + dc, 2)
        return (lax.rem(nx, 2), ((nz * 4 + ny) * 2 + nx // 2) * 2 + nc)

    xp, xm, x2 = at(dx=1), at(dx=-1), at(dx=2)
    yd = (at(dy=1), at(dy=-1))
    zd = (at(dz=1), at(dz=-1))
    sib = at(dc=1)

    barrier = pltpu.get_barrier_semaphore()
    for peer in (xp, xm, x2, yd[0], yd[1], zd[0], zd[1], sib):
        pl.semaphore_signal(barrier, 1, device_id=peer, device_id_type=MESH)

    fetch = pltpu.make_async_copy(weight.at[0], w_buf, w_sem)
    fetch.start()

    def move(src, dst, send, recv, peer):
        return pltpu.make_async_remote_copy(
            src_ref=src, dst_ref=dst, send_sem=send, recv_sem=recv, device_id=peer, device_id_type=MESH
        )

    def rows(start, n=64):
        return pl.ds(start, n)

    def i_row(rel, q, half):
        return Y_SLOT[rel] * 256 + q * 128 + half * 64

    def t_row(rel, half):
        return Z_SLOT[rel] * 128 + half * 64

    values = pooled[0].astype(F32)
    center = values - jnp.mean(values, axis=-1, keepdims=True)
    spread = jnp.mean(center * center, axis=-1, keepdims=True)
    normed = (center * lax.rsqrt(spread + 1e-06) * gain[...]).astype(BF)
    fetch.wait()
    head = jnp.dot(normed, w_buf[...], preferred_element_type=F32)
    length = jnp.sum(head * head, axis=-1, keepdims=True)
    emb[...] = (head * lax.rsqrt(length + 1e-06)).astype(BF)
    pl.semaphore_wait(barrier, 8)

    def x_copies():
        res = []
        for half in (0, 1):
            for k, (peer, q) in enumerate(((xp, 0), (xm, 1), (x2, 1))):
                dst = img.at[rows(i_row(0, q, half))]
                res.append(move(emb.at[rows(half * 64)], dst, sx.at[k, half], rx.at[q, half], peer))
        return res

    def x_wait(q, half):
        dst = img.at[rows(i_row(0, q, half))]
        move(emb.at[rows(half * 64)], dst, sx.at[0, half], rx.at[q, half], xp).wait_recv()

    def tx_copies():
        return [
            move(emb.at[rows(half * 64)], txt.at[rows(t_row(0, half))], stx.at[half], rtx.at[half], xm)
            for half in (0, 1)
        ]

    def y_copy(d, q, half, dist):
        sign = 1 - 2 * d
        idx = q * 2 + half if dist == 1 else 4 + q
        src_rel = 0 if dist == 1 else -sign
        dst_rel = -sign if dist == 1 else 2
        return move(
            img.at[rows(i_row(src_rel, q, half))], img.at[rows(i_row(dst_rel, q, half))],
            sy.at[d, idx], ry.at[d, idx], yd[d],
        )

    def z_rel(d, dist):
        rel = -dist if d == 0 else dist
        return 4 if rel == -4 else rel

    def z_copy(d, i):
        half, dist = Z_OUT[i]
        half = half ^ d
        src = txt.at[rows(t_row(z_rel(d, dist - 1), half))]
        dst = txt.at[rows(t_row(z_rel(d, dist), half))]
        return move(src, dst, sz.at[d, i], rz.at[d, i], zd[d])

    def s_copy(n, rel, half):
        part = txt.at[rows(t_row(rel, half))]
        return move(part, part, ss.at[n], rs.at[n], sib)

    S_LIST = [(0, 0), (0, 1)] + [(z_rel(d, Z_OUT[i][1]), Z_OUT[i][0] ^ d) for i in range(7) for d in (0, 1)]

    @pl.when(is_img)
    def _():
        for copy in x_copies():
            copy.start()
        img[256:384, :] = emb[...]

    @pl.when(jnp.logical_and(is_txt, guest))
    def _():
        for copy in tx_copies():
            copy.start()

    @pl.when(jnp.logical_and(is_txt, home))
    def _():
        txt[896:1024, :] = emb[...]

    def z_own():
        for i in (0, 1):
            for d in (0, 1):
                z_copy(d, i).start()
        for n in (0, 1):
            s_copy(n, *S_LIST[n]).start()

    @pl.when(jnp.logical_and(is_txt, home))
    def _():
        z_own()

    @pl.when(is_txt)
    def _():
        x_wait(0, 0)
        x_wait(0, 1)

    y_copy(0, 0, 0, 1).start()
    y_copy(1, 0, 1, 1).start()

    for rel, slot in Z_SLOT.items():
        row = ((lax.rem(z + rel + 8, 8) * 4 + y) * 2 + h) * 2 + t
        txt_ids[:, slot * 128 : slot * 128 + 128] = jnp.broadcast_to(ids[pl.ds(row, 1), :], (8, 128))
    for rel, slot in Y_SLOT.items():
        for q in (0, 1):
            row = ((z * 4 + lax.rem(y + rel + 4, 4)) * 2 + lax.rem(h + q, 2)) * 2 + c
            block = jnp.broadcast_to(ids[pl.ds(row, 1), :], (128, 128))
            start = slot * 256 + q * 128
            img_ids[start : start + 128, :] = block.T

    @pl.when(jnp.logical_and(is_img, home))
    def _():
        for copy in tx_copies():
            copy.wait_recv()
        z_own()

    x_wait(1, 0)
    x_wait(1, 1)
    y_copy(0, 1, 0, 1).start()
    y_copy(1, 1, 1, 1).start()

    def z_step(i):
        for d in (0, 1):
            z_copy(d, i).wait_recv()
            if i + 2 < 7:
                z_copy(d, i + 2).start()
            n = 2 + i * 2 + d
            s_copy(n, *S_LIST[n]).start()

    def z_steps(*steps):
        @pl.when(home)
        def _():
            for i in steps:
                z_step(i)

    def y_relay(q):
        for d in (0, 1):
            y_copy(d, q, d, 1).wait_recv()
            y_copy(d, q, d, 2).start()

    z_steps(0, 1)
    y_relay(0)
    z_steps(2)
    y_relay(1)
    for q in (0, 1):
        for d in (0, 1):
            y_copy(d, q, 1 - d, 1).start()
    z_steps(3, 4, 5, 6)

    @pl.when(guest)
    def _():
        for n in range(16):
            s_copy(n, *S_LIST[n]).wait_recv()

    scale = jnp.exp(log_scale[...])
    shift = bias[...]

    def tile(slot):
        part = pl.ds(slot * 256, 256)
        logits = scale * lax.dot_general(
            img[part, :], txt[...], (((1,), (1,)), ((), ())), preferred_element_type=F32
        ) + shift
        same = img_ids[part, 0:1] == txt_ids[0:1, :]
        weight_ = 1.0 / (1.0 + jnp.exp(jnp.minimum(jnp.where(same, logits, -logits), 88.0)))
        coef[part, :] = jnp.where(same, -weight_, weight_).astype(BF)
        g_img[part, :] = jnp.dot(coef[part, :], txt[...], preferred_element_type=F32)

    def yr_copy(d, q, half, dist):
        sign = 1 - 2 * d
        if dist == 2:
            return move(
                s_img.at[rows(i_row(2, q, half))], r_y2.at[rows((d * 2 + q) * 64)],
                syr.at[d, 4 + q], ryr.at[d, 4 + q], yd[d],
            )
        idx = q * 2 + half
        return move(
            s_img.at[rows(i_row(sign, q, half))], r_y1.at[rows((d * 4 + idx) * 64)],
            syr.at[d, idx], ryr.at[d, idx], yd[d],
        )

    for d in (0, 1):
        for q in (0, 1):
            y_copy(d, q, d, 2).wait_recv()
    tile(0)
    s_img[0:256, :] = g_img[0:256, :].astype(BF)
    for q in (0, 1):
        for d in (0, 1):
            yr_copy(d, q, d, 2).start()
    tile(1)

    def first_units():
        g_txt[...] = lax.dot_general(
            coef[0:512, :], img[0:512, :], (((0,), (0,)), ((), ())), preferred_element_type=F32
        )

    first_units()

    def y_side(d):
        sign = 1 - 2 * d
        slot = Y_SLOT[sign]
        tile(slot)
        for q in (0, 1):
            yr_copy(d, q, d, 2).wait_recv()
            for half in (0, 1):
                start = i_row(sign, q, half)
                total = g_img[start : start + 64, :]
                if half == d:
                    total = total + r_y2[(d * 2 + q) * 64 : (d * 2 + q) * 64 + 64, :].astype(F32)
                s_img[start : start + 64, :] = total.astype(BF)
                yr_copy(d, q, half, 1).start()

    for d in (0, 1):
        for q in (0, 1):
            y_copy(d, q, 1 - d, 1).wait_recv()
    y_side(0)
    y_side(1)

    def s2_copy(u):
        part = pl.ds(*UNITS[u])
        return move(s_txt.at[part], r_sib.at[part], ss2.at[u], rs2.at[u], sib)

    for u, (start, n) in enumerate(UNITS):
        g_txt[start : start + n, :] += lax.dot_general(
            coef[512:1024, start : start + n], img[512:1024, :], (((0,), (0,)), ((), ())), preferred_element_type=F32
        )

        @pl.when(guest)
        def _():
            s_txt[start : start + n, :] = g_txt[start : start + n, :].astype(BF)
            s2_copy(u).start()

    def zr_copy(d, i):
        half, dist = Z_BACK[i]
        half = half ^ d
        rel = dist if d == 0 else -dist
        rel = 4 if rel == -4 else rel
        return move(
            s_txt.at[rows(t_row(rel, half))], r_z.at[rows((d * 7 + i) * 64)], szr.at[d, i], rzr.at[d, i], zd[d]
        )

    def zr_take(d, i):
        zr_copy(d, i - 2).wait_recv()
        return r_z[(d * 7 + i - 2) * 64 : (d * 7 + i - 2) * 64 + 64, :].astype(F32)

    def zr_send(i):
        for d in (0, 1):
            half, dist = Z_BACK[i]
            half = half ^ d
            rel = dist if d == 0 else -dist
            start = t_row(4 if rel == -4 else rel, half)
            total = g_txt[start : start + 64, :] + r_sib[start : start + 64, :].astype(F32)
            if i >= 2:
                total = total + zr_take(d, i)
            s_txt[start : start + 64, :] = total.astype(BF)
            zr_copy(d, i).start()

    def xr_copies(q, half):
        src = s_x.at[rows(q * 128 + half * 64)]
        if q == 0:
            return [(is_txt, move(src, r_x.at[rows(half * 64)], sxr.at[q, half], rxr.at[0, half], xm))]
        return [
            (is_txt, move(src, r_x.at[rows(128 + half * 64)], sxr.at[q, half], rxr.at[1, half], xp)),
            (is_img, move(src, r_x.at[rows(256 + half * 64)], sxr.at[q, half], rxr.at[2, half], x2)),
        ]

    def y_final(q, half):
        for d in (0, 1):
            yr_copy(d, q, half, 1).wait_recv()
        start = i_row(0, q, half)
        k = (q * 2 + half) * 64
        total = g_img[start : start + 64, :] + r_y1[k : k + 64, :].astype(F32) + r_y1[256 + k : 256 + k + 64, :].astype(F32)
        if q == 0:
            g_img[start : start + 64, :] = total
        s_x[q * 128 + half * 64 : q * 128 + half * 64 + 64, :] = total.astype(BF)
        for cond, copy in xr_copies(q, half):
            pl.when(cond)(copy.start)

    def zr_steps(*steps):
        @pl.when(home)
        def _():
            for i in steps:
                zr_send(i)

    @pl.when(home)
    def _():
        s2_copy(0).wait_recv()

    zr_steps(0, 1)

    @pl.when(home)
    def _():
        s2_copy(1).wait_recv()
        s2_copy(2).wait_recv()

    zr_steps(2)
    y_final(0, 0)
    zr_steps(3)
    y_final(0, 1)
    zr_steps(4)
    y_final(1, 0)
    zr_steps(5)
    y_final(1, 1)
    zr_steps(6)

    def f_copies():
        return [
            move(s_txt.at[rows(896 + half * 64)], r_fin.at[rows(half * 64)], sf.at[half], rf.at[half], xp)
            for half in (0, 1)
        ]

    @pl.when(home)
    def _():
        for half in (1, 0):
            start = t_row(0, half)
            total = g_txt[start : start + 64, :] + r_sib[start : start + 64, :].astype(F32)
            for d in (0, 1):
                i = 7 if half ^ d == 1 else 8
                total = total + zr_take(d, i)

            @pl.when(is_txt)
            def _():
                out[0, half * 64 : half * 64 + 64, :] = total

            @pl.when(is_img)
            def _():
                s_txt[start : start + 64, :] = total.astype(BF)
                f_copies()[half].start()

    @pl.when(is_img)
    def _():
        for half in (0, 1):
            for k in range(3):
                part = r_x.at[rows(k * 128 + half * 64)]
                move(part, part, sxr.at[0, half], rxr.at[k, half], xp).wait_recv()
            total = g_img[i_row(0, 0, half) : i_row(0, 0, half) + 64, :]
            for k in range(3):
                total = total + r_x[k * 128 + half * 64 : k * 128 + half * 64 + 64, :].astype(F32)
            out[0, half * 64 : half * 64 + 64, :] = total

    @pl.when(jnp.logical_and(is_txt, guest))
    def _():
        for copy in f_copies():
            copy.wait_recv()
        out[0, :, :] = r_fin[...].astype(F32)

    @pl.when(is_img)
    def _():
        for copy in x_copies():
            copy.wait_send()

    @pl.when(jnp.logical_and(is_txt, guest))
    def _():
        for copy in tx_copies():
            copy.wait_send()

    for d in (0, 1):
        for q in (0, 1):
            for half in (0, 1):
                y_copy(d, q, half, 1).wait_send()
                yr_copy(d, q, half, 1).wait_send()
            y_copy(d, q, d, 2).wait_send()
            yr_copy(d, q, d, 2).wait_send()

    @pl.when(home)
    def _():
        for i in range(7):
            for d in (0, 1):
                z_copy(d, i).wait_send()
                zr_copy(d, i).wait_send()
        for n in range(16):
            s_copy(n, *S_LIST[n]).wait_send()

    @pl.when(guest)
    def _():
        for u in range(3):
            s2_copy(u).wait_send()

    for q in (0, 1):
        for half in (0, 1):
            for cond, copy in xr_copies(q, half):
                pl.when(cond)(copy.wait_send)

    @pl.when(jnp.logical_and(is_img, home))
    def _():
        for copy in f_copies():
            copy.wait_send()


def on_device(pooled, final_gain, head_weight, pair_ids, log_scale, bias):
    n, d = pooled.shape[1:]
    vmem = pl.BlockSpec(memory_space=pltpu.VMEM)
    buf = lambda r, kind=BF: pltpu.VMEM((r, d), kind)
    dma = pltpu.SemaphoreType.DMA
    return pl.pallas_call(
        kernel,
        out_shape=jax.ShapeDtypeStruct((1, n, d), F32),
        in_specs=[vmem, vmem, pl.BlockSpec(memory_space=pl.ANY), vmem, vmem, vmem],
        out_specs=vmem,
        scratch_shapes=[
            buf(d), buf(128), buf(1024), buf(1024), pltpu.VMEM((1024, 1024), BF), buf(1024, F32), buf(1024, F32),
            buf(1024), buf(256), buf(1024), buf(1024), buf(14 * 64), buf(4 * 64), buf(8 * 64), buf(6 * 64), buf(128),
            pltpu.VMEM((1024, 128), jnp.int32), pltpu.VMEM((8, 1024), jnp.int32),
            dma, dma((3, 2)), dma((2, 2)), dma((2,)), dma((2,)), dma((2, 6)), dma((2, 6)), dma((2, 7)), dma((2, 7)),
            dma((16,)), dma((16,)), dma((3,)), dma((3,)), dma((2, 7)), dma((2, 7)), dma((2, 6)), dma((2, 6)),
            dma((2, 2)), dma((3, 2)), dma((2,)), dma((2,)),
        ],
        compiler_params=pltpu.CompilerParams(collective_id=0, has_side_effects=True, vmem_limit_bytes=60 * 2**20),
        name="towers",
    )(pooled, final_gain, head_weight, pair_ids.reshape(128, 128), log_scale.reshape(1, 1), bias.reshape(1, 1))


def solution(mesh):
    placed = (P("tower", "blk", None), P("tower", None), P("tower", None, None), P(), P(), P())
    return jax.shard_map(
        on_device, mesh=mesh, in_specs=placed, out_specs=P("tower", "blk", None), check_vma=False
    )
```

```python
import jax
import jax.numpy as jnp
from jax import lax
from jax.experimental import pallas as pl
from jax.experimental.pallas import tpu as pltpu
from jax.sharding import PartitionSpec as P

MESH = pl.DeviceIdType.MESH
BF = jnp.bfloat16
F32 = jnp.float32

Y_SLOT = {2: 0, 0: 1, 1: 2, -1: 3}
Z_SLOT = {4: 0, 3: 1, -3: 2, 2: 3, -2: 4, 1: 5, -1: 6, 0: 7}
UNITS = ((0, 384), (384, 256), (640, 384))
Z_OUT = tuple([(k, dist) for dist in (1, 2, 3) for k in range(4)] + [(k + 2 * d, 4) for k in (0, 1)] for d in (0, 1))
Z_BACK = ((0, 4), (1, 4)) + tuple((k, dist) for dist in (3, 2, 1) for k in (2, 3, 0, 1))


def kernel(
    pooled_hbm, gain_hbm, weight, ids_hbm, log_scale, bias, out,
    pooled, gain, ids, w_buf, emb, img, txt, coef, g_img, g_txt, s_img, s_x, s_txt, r_sib, r_z, r_y2, r_y1, r_x, r_fin,
    img_ids, txt_ids,
    in_sem, sx, rx, stx, rtx, sy, ry, sz, rz, ss, rs, ss2, rs2, szr, rzr, syr, ryr, sxr, rxr, sf, rf,
):
    t = lax.axis_index("tower")
    b = lax.axis_index("blk")
    c = lax.rem(b, 2)
    h = lax.rem(b // 2, 2)
    y = lax.rem(b // 4, 4)
    z = b // 16
    x = h * 2 + t
    is_img = t == 0
    is_txt = t == 1
    home = c == t
    guest = c != t

    def at(dx=0, dy=0, dz=0, dc=0):
        nx = lax.rem(x + dx + 4, 4)
        ny = lax.rem(y + dy + 4, 4)
        nz = lax.rem(z + dz + 8, 8)
        nc = lax.rem(c + dc, 2)
        return (lax.rem(nx, 2), ((nz * 4 + ny) * 2 + nx // 2) * 2 + nc)

    xp, xm, x2 = at(dx=1), at(dx=-1), at(dx=2)
    yd = (at(dy=1), at(dy=-1))
    zd = (at(dz=1), at(dz=-1))
    sib = at(dc=1)

    fetches = [
        pltpu.make_async_copy(a, b, in_sem.at[n])
        for n, (a, b) in enumerate(
            ((pooled_hbm.at[0], pooled), (gain_hbm, gain), (weight.at[0], w_buf), (ids_hbm, ids))
        )
    ]
    for fetch in fetches:
        fetch.start()

    barrier = pltpu.get_barrier_semaphore()
    for peer in (xp, xm, x2, yd[0], yd[1], zd[0], zd[1], sib):
        pl.semaphore_signal(barrier, 1, device_id=peer, device_id_type=MESH)

    def move(src, dst, send, recv, peer):
        return pltpu.make_async_remote_copy(
            src_ref=src, dst_ref=dst, send_sem=send, recv_sem=recv, device_id=peer, device_id_type=MESH
        )

    def rows(start, n=64):
        return pl.ds(start, n)

    def i_row(rel, q, half):
        return Y_SLOT[rel] * 256 + q * 128 + half * 64

    def t_row(rel, k):
        return Z_SLOT[rel] * 128 + k * 32

    fetches[0].wait()
    fetches[1].wait()
    values = pooled[...].astype(F32)
    center = values - jnp.mean(values, axis=-1, keepdims=True)
    spread = jnp.mean(center * center, axis=-1, keepdims=True)
    normed = (center * lax.rsqrt(spread + 1e-06) * gain[...]).astype(BF)
    fetches[2].wait()
    head = jnp.dot(normed, w_buf[...], preferred_element_type=F32)
    length = jnp.sum(head * head, axis=-1, keepdims=True)
    emb[...] = (head * lax.rsqrt(length + 1e-06)).astype(BF)
    pl.semaphore_wait(barrier, 8)

    def x_copies():
        res = []
        for half in (0, 1):
            for k, (peer, q) in enumerate(((xp, 0), (xm, 1), (x2, 1))):
                dst = img.at[rows(i_row(0, q, half))]
                res.append(move(emb.at[rows(half * 64)], dst, sx.at[k, half], rx.at[q, half], peer))
        return res

    def x_wait(q, half):
        dst = img.at[rows(i_row(0, q, half))]
        move(emb.at[rows(half * 64)], dst, sx.at[0, half], rx.at[q, half], xp).wait_recv()

    def tx_copy(k):
        return move(emb.at[rows(k * 32, 32)], txt.at[rows(t_row(0, k), 32)], stx.at[k], rtx.at[k], xm)

    def y_copy(d, q, half, dist):
        sign = 1 - 2 * d
        idx = q * 2 + half if dist == 1 else 4 + q
        src_rel = 0 if dist == 1 else -sign
        dst_rel = -sign if dist == 1 else 2
        return move(
            img.at[rows(i_row(src_rel, q, half))], img.at[rows(i_row(dst_rel, q, half))],
            sy.at[d, idx], ry.at[d, idx], yd[d],
        )

    def z_rel(d, dist):
        rel = -dist if d == 0 else dist
        return 4 if rel == -4 else rel

    def z_copy(d, i):
        k, dist = Z_OUT[d][i]
        src = txt.at[rows(t_row(z_rel(d, dist - 1), k), 32)]
        dst = txt.at[rows(t_row(z_rel(d, dist), k), 32)]
        return move(src, dst, sz.at[d, i], rz.at[d, i], zd[d])

    S_LIST = [(0, 0), (0, 1)] + [
        (z_rel(d, Z_OUT[d][i][1]), Z_OUT[d][i][0] // 2) for i in range(0, 14, 2) for d in (0, 1)
    ]

    def s_copy(n):
        rel, half = S_LIST[n]
        part = txt.at[rows(t_row(rel, half * 2))]
        return move(part, part, ss.at[n], rs.at[n], sib)

    @pl.when(is_img)
    def _():
        for copy in x_copies():
            copy.start()
        img[256:384, :] = emb[...]

    @pl.when(jnp.logical_and(is_txt, guest))
    def _():
        for k in range(4):
            tx_copy(k).start()

    @pl.when(jnp.logical_and(is_txt, home))
    def _():
        txt[896:1024, :] = emb[...]
        for k in range(4):
            for d in (0, 1):
                z_copy(d, k).start()
        for n in (0, 1):
            s_copy(n).start()

    def y_pair(q, half):
        for d in (0, 1):
            y_copy(d, q, half, 1).start()

    @pl.when(is_img)
    def _():
        y_pair(0, 0)
        y_pair(0, 1)

    fetches[3].wait()
    for rel, slot in Z_SLOT.items():
        row = ((lax.rem(z + rel + 8, 8) * 4 + y) * 2 + h) * 2 + t
        txt_ids[:, slot * 128 : slot * 128 + 128] = jnp.broadcast_to(ids[pl.ds(row, 1), :], (8, 128))
    for rel, slot in Y_SLOT.items():
        for q in (0, 1):
            row = ((z * 4 + lax.rem(y + rel + 4, 4)) * 2 + lax.rem(h + q, 2)) * 2 + c
            block = jnp.broadcast_to(ids[pl.ds(row, 1), :], (128, 128))
            start = slot * 256 + q * 128
            img_ids[start : start + 128, :] = block.T

    @pl.when(jnp.logical_and(is_img, home))
    def _():
        for k in range(4):
            tx_copy(k).wait_recv()
            for d in (0, 1):
                z_copy(d, k).start()
        for n in (0, 1):
            s_copy(n).start()

    def z_steps(*steps):
        @pl.when(home)
        def _():
            for i in steps:
                for d in (0, 1):
                    z_copy(d, i).wait_recv()
                    k, dist = Z_OUT[d][i]
                    if (k, dist + 1) in Z_OUT[d]:
                        z_copy(d, Z_OUT[d].index((k, dist + 1))).start()
                    if i % 2:
                        s_copy(2 + i // 2 * 2 + d).start()

    def y_relay(q):
        for d in (0, 1):
            y_copy(d, q, d, 1).wait_recv()
            y_copy(d, q, d, 2).start()

    z_steps(0, 1, 2, 3)

    @pl.when(is_img)
    def _():
        x_wait(1, 0)
        y_copy(0, 1, 0, 1).start()
        x_wait(1, 1)
        y_copy(1, 1, 1, 1).start()

    @pl.when(is_txt)
    def _():
        x_wait(0, 0)
        y_pair(0, 0)
        x_wait(1, 0)
        y_copy(0, 1, 0, 1).start()
        x_wait(0, 1)
        y_pair(0, 1)
        x_wait(1, 1)
        y_copy(1, 1, 1, 1).start()

    y_relay(0)
    z_steps(4, 5, 6, 7)
    y_relay(1)
    for d in (0, 1):
        y_copy(d, 1, 1 - d, 1).start()
    z_steps(*range(8, 14))

    @pl.when(guest)
    def _():
        for n in range(16):
            s_copy(n).wait_recv()

    scale = jnp.exp(jnp.full((1, 1), log_scale[0], F32))
    shift = bias[0]

    def tile(slot):
        part = pl.ds(slot * 256, 256)
        logits = scale * lax.dot_general(
            img[part, :], txt[...], (((1,), (1,)), ((), ())), preferred_element_type=F32
        ) + shift
        same = img_ids[part, 0:1] == txt_ids[0:1, :]
        weight_ = 1.0 / (1.0 + jnp.exp(jnp.minimum(jnp.where(same, logits, -logits), 88.0)))
        coef[part, :] = jnp.where(same, -weight_, weight_).astype(BF)
        g_img[part, :] = jnp.dot(coef[part, :], txt[...], preferred_element_type=F32)

    def yr_copy(d, q, half, dist):
        sign = 1 - 2 * d
        if dist == 2:
            return move(
                s_img.at[rows(i_row(2, q, half))], r_y2.at[rows((d * 2 + q) * 64)],
                syr.at[d, 4 + q], ryr.at[d, 4 + q], yd[d],
            )
        idx = q * 2 + half
        return move(
            s_img.at[rows(i_row(sign, q, half))], r_y1.at[rows((d * 4 + idx) * 64)],
            syr.at[d, idx], ryr.at[d, idx], yd[d],
        )

    tile(1)
    for d in (0, 1):
        for q in (0, 1):
            y_copy(d, q, d, 2).wait_recv()
    tile(0)
    s_img[0:256, :] = g_img[0:256, :].astype(BF)
    for q in (0, 1):
        for d in (0, 1):
            yr_copy(d, q, d, 2).start()
    for d in (0, 1):
        for q in (0, 1):
            y_copy(d, q, 1 - d, 1).wait_recv()
    tile(2)
    tile(3)

    def y_sums(d):
        sign = 1 - 2 * d
        for q in (0, 1):
            yr_copy(d, q, d, 2).wait_recv()
            for half in (0, 1):
                start = i_row(sign, q, half)
                total = g_img[start : start + 64, :]
                if half == d:
                    total = total + r_y2[(d * 2 + q) * 64 : (d * 2 + q) * 64 + 64, :].astype(F32)
                s_img[start : start + 64, :] = total.astype(BF)
                yr_copy(d, q, half, 1).start()

    def s2_copy(u):
        part = pl.ds(*UNITS[u])
        return move(s_txt.at[part], r_sib.at[part], ss2.at[u], rs2.at[u], sib)

    def text_dot(start, n):
        return lax.dot_general(
            coef[:, start : start + n], img[...], (((0,), (0,)), ((), ())), preferred_element_type=F32
        )

    def text_unit(u):
        start, n = UNITS[u]
        g_txt[start : start + n, :] = text_dot(start, n)

        @pl.when(guest)
        def _():
            s_txt[start : start + n, :] = g_txt[start : start + n, :].astype(BF)
            s2_copy(u).start()

    def back(d, i):
        k, dist = Z_BACK[i]
        rel = dist if d == 0 or dist == 4 else -dist
        return t_row(rel, k ^ (2 * d))

    def zr_copy(d, i):
        return move(
            s_txt.at[rows(back(d, i), 32)], r_z.at[rows((d * 14 + i) * 32, 32)], szr.at[d, i], rzr.at[d, i], zd[d]
        )

    def zr_take(d, i):
        zr_copy(d, i).wait_recv()
        return r_z[(d * 14 + i) * 32 : (d * 14 + i) * 32 + 32, :].astype(F32)

    def zr_steps(*steps):
        @pl.when(home)
        def _():
            for i in steps:
                for d in (0, 1):
                    start = back(d, i)
                    total = g_txt[start : start + 32, :] + r_sib[start : start + 32, :].astype(F32)
                    if i >= 4:
                        total = total + zr_take(d, i - 4)
                    s_txt[start : start + 32, :] = total.astype(BF)
                    zr_copy(d, i).start()

    def xr_copies(q, half):
        src = s_x.at[rows(q * 128 + half * 64)]
        if q == 0:
            return [(is_txt, move(src, r_x.at[rows(half * 64)], sxr.at[q, half], rxr.at[0, half], xm))]
        return [
            (is_txt, move(src, r_x.at[rows(128 + half * 64)], sxr.at[q, half], rxr.at[1, half], xp)),
            (is_img, move(src, r_x.at[rows(256 + half * 64)], sxr.at[q, half], rxr.at[2, half], x2)),
        ]

    def y_final(q, half):
        for d in (0, 1):
            yr_copy(d, q, half, 1).wait_recv()
        start = i_row(0, q, half)
        k = (q * 2 + half) * 64
        total = g_img[start : start + 64, :] + r_y1[k : k + 64, :].astype(F32) + r_y1[256 + k : 256 + k + 64, :].astype(F32)
        if q == 0:
            g_img[start : start + 64, :] = total
        s_x[q * 128 + half * 64 : q * 128 + half * 64 + 64, :] = total.astype(BF)
        for cond, copy in xr_copies(q, half):
            pl.when(cond)(copy.start)

    def s2_wait(*units):
        @pl.when(home)
        def _():
            for u in units:
                s2_copy(u).wait_recv()

    text_unit(0)
    y_sums(0)
    y_sums(1)
    s2_wait(0)
    zr_steps(0, 1, 2, 3)
    text_unit(1)
    text_unit(2)
    s2_wait(1, 2)
    zr_steps(4, 5, 6, 7)
    y_final(0, 0)
    y_final(0, 1)
    zr_steps(8, 9)
    y_final(1, 0)
    zr_steps(10, 11)
    y_final(1, 1)
    zr_steps(12, 13)

    def f_copy(k):
        return move(s_txt.at[rows(t_row(0, k), 32)], r_fin.at[rows(k * 32, 32)], sf.at[k], rf.at[k], xp)

    @pl.when(home)
    def _():
        for k in (2, 3, 0, 1):
            start = t_row(0, k)
            total = g_txt[start : start + 32, :] + r_sib[start : start + 32, :].astype(F32)
            for d in (0, 1):
                total = total + zr_take(d, 10 + ((2, 3, 0, 1).index(k ^ (2 * d))))

            @pl.when(is_txt)
            def _():
                out[0, k * 32 : k * 32 + 32, :] = total

            @pl.when(is_img)
            def _():
                s_txt[start : start + 32, :] = total.astype(BF)
                f_copy(k).start()

    @pl.when(is_img)
    def _():
        for half in (0, 1):
            for k in range(3):
                part = r_x.at[rows(k * 128 + half * 64)]
                move(part, part, sxr.at[0, half], rxr.at[k, half], xp).wait_recv()
            total = g_img[i_row(0, 0, half) : i_row(0, 0, half) + 64, :]
            for k in range(3):
                total = total + r_x[k * 128 + half * 64 : k * 128 + half * 64 + 64, :].astype(F32)
            out[0, half * 64 : half * 64 + 64, :] = total

    @pl.when(jnp.logical_and(is_txt, guest))
    def _():
        for k in (2, 3, 0, 1):
            f_copy(k).wait_recv()
            out[0, k * 32 : k * 32 + 32, :] = r_fin[k * 32 : k * 32 + 32, :].astype(F32)

    @pl.when(is_img)
    def _():
        for copy in x_copies():
            copy.wait_send()

    @pl.when(jnp.logical_and(is_txt, guest))
    def _():
        for k in range(4):
            tx_copy(k).wait_send()

    for d in (0, 1):
        for q in (0, 1):
            for half in (0, 1):
                y_copy(d, q, half, 1).wait_send()
                yr_copy(d, q, half, 1).wait_send()
            y_copy(d, q, d, 2).wait_send()
            yr_copy(d, q, d, 2).wait_send()

    @pl.when(home)
    def _():
        for i in range(14):
            for d in (0, 1):
                z_copy(d, i).wait_send()
                zr_copy(d, i).wait_send()
        for n in range(16):
            s_copy(n).wait_send()

    @pl.when(guest)
    def _():
        for u in range(3):
            s2_copy(u).wait_send()

    for q in (0, 1):
        for half in (0, 1):
            for cond, copy in xr_copies(q, half):
                pl.when(cond)(copy.wait_send)

    @pl.when(jnp.logical_and(is_img, home))
    def _():
        for k in range(4):
            f_copy(k).wait_send()


def on_device(pooled, final_gain, head_weight, pair_ids, log_scale, bias):
    n, d = pooled.shape[1:]
    hbm = pl.BlockSpec(memory_space=pl.ANY)
    smem = pl.BlockSpec(memory_space=pltpu.SMEM)
    buf = lambda r, kind=BF: pltpu.VMEM((r, d), kind)
    dma = pltpu.SemaphoreType.DMA
    return pl.pallas_call(
        kernel,
        out_shape=jax.ShapeDtypeStruct((1, n, d), F32),
        in_specs=[hbm, hbm, hbm, hbm, smem, smem],
        out_specs=pl.BlockSpec(memory_space=pltpu.VMEM),
        scratch_shapes=[
            buf(n), buf(1, F32), pltpu.VMEM((128, 128), jnp.int32), buf(d), buf(128), buf(1024), buf(1024), pltpu.VMEM((1024, 1024), BF), buf(1024, F32), buf(1024, F32),
            buf(1024), buf(256), buf(1024), buf(1024), buf(14 * 64), buf(4 * 64), buf(8 * 64), buf(6 * 64), buf(128),
            pltpu.VMEM((1024, 128), jnp.int32), pltpu.VMEM((8, 1024), jnp.int32),
            dma((4,)), dma((3, 2)), dma((2, 2)), dma((4,)), dma((4,)), dma((2, 6)), dma((2, 6)), dma((2, 14)), dma((2, 14)),
            dma((16,)), dma((16,)), dma((3,)), dma((3,)), dma((2, 14)), dma((2, 14)), dma((2, 6)), dma((2, 6)),
            dma((2, 2)), dma((3, 2)), dma((4,)), dma((4,)),
        ],
        compiler_params=pltpu.CompilerParams(collective_id=0, has_side_effects=True, vmem_limit_bytes=60 * 2**20),
        name="towers",
    )(pooled, final_gain, head_weight, pair_ids.reshape(128, 128), log_scale, bias)


def solution(mesh):
    placed = (P("tower", "blk", None), P("tower", None), P("tower", None, None), P(), P(), P())
    return jax.shard_map(
        on_device, mesh=mesh, in_specs=placed, out_specs=P("tower", "blk", None), check_vma=False
    )
```

```python
import jax
import jax.numpy as jnp
from jax import lax
from jax.experimental import pallas as pl
from jax.experimental.pallas import tpu as pltpu
from jax.sharding import PartitionSpec as P

MESH = pl.DeviceIdType.MESH
BF = jnp.bfloat16
F32 = jnp.float32

I_SLOT = {(2, 0): 0, (2, 1): 1, (0, 0): 2, (0, 1): 3, (1, 0): 4, (-1, 0): 5, (1, 1): 6, (-1, 1): 7}
Z_SLOT = {4: 0, 3: 1, -3: 2, 2: 3, -2: 4, 1: 5, -1: 6, 0: 7}
UNITS = ((0, 384), (384, 256), (640, 384))
Z_OUT = tuple([(k, dist) for dist in (1, 2, 3) for k in range(4)] + [(k + 2 * d, 4) for k in (0, 1)] for d in (0, 1))
Z_BACK = ((0, 4), (1, 4)) + tuple((k, dist) for dist in (3, 2, 1) for k in (2, 3, 0, 1))


def kernel(
    pooled_hbm, gain_hbm, weight, ids_hbm, log_scale, bias, out,
    pooled, gain, ids, w_buf, emb, img, txt, coef, g_img, g_txt, s_img, s_x, s_txt, r_sib, r_z, r_y2, r_y1, r_x, r_fin,
    img_ids, txt_ids,
    in_sem, sx, rx, sxw, rxw, stx, rtx, sy, ry, sz, rz, ss, rs, ss2, rs2, szr, rzr, syr, ryr, sxr, rxr, sf, rf,
):
    t = lax.axis_index("tower")
    b = lax.axis_index("blk")
    c = lax.rem(b, 2)
    h = lax.rem(b // 2, 2)
    y = lax.rem(b // 4, 4)
    z = b // 16
    x = h * 2 + t
    is_img = t == 0
    is_txt = t == 1
    home = c == t
    guest = c != t

    def at(dx=0, dy=0, dz=0, dc=0):
        nx = lax.rem(x + dx + 4, 4)
        ny = lax.rem(y + dy + 4, 4)
        nz = lax.rem(z + dz + 8, 8)
        nc = lax.rem(c + dc, 2)
        return (lax.rem(nx, 2), ((nz * 4 + ny) * 2 + nx // 2) * 2 + nc)

    xp, xm, x2 = at(dx=1), at(dx=-1), at(dx=2)
    yd = (at(dy=1), at(dy=-1))
    zd = (at(dz=1), at(dz=-1))
    sib = at(dc=1)

    fetches = [
        pltpu.make_async_copy(a, b, in_sem.at[n])
        for n, (a, b) in enumerate(
            ((pooled_hbm.at[0], pooled), (gain_hbm, gain), (weight.at[0], w_buf), (ids_hbm, ids))
        )
    ]
    for fetch in fetches:
        fetch.start()

    barrier = pltpu.get_barrier_semaphore()
    for peer in (xp, xm, x2, yd[0], yd[1], zd[0], zd[1], sib):
        pl.semaphore_signal(barrier, 1, device_id=peer, device_id_type=MESH)

    def move(src, dst, send, recv, peer):
        return pltpu.make_async_remote_copy(
            src_ref=src, dst_ref=dst, send_sem=send, recv_sem=recv, device_id=peer, device_id_type=MESH
        )

    def rows(start, n=64):
        return pl.ds(start, n)

    def i_row(rel, q, half):
        return I_SLOT[rel, q] * 128 + half * 64

    def t_row(rel, k):
        return Z_SLOT[rel] * 128 + k * 32

    fetches[0].wait()
    fetches[1].wait()
    values = pooled[...].astype(F32)
    center = values - jnp.mean(values, axis=-1, keepdims=True)
    spread = jnp.mean(center * center, axis=-1, keepdims=True)
    normed = (center * lax.rsqrt(spread + 1e-06) * gain[...]).astype(BF)
    fetches[2].wait()
    head = jnp.dot(normed, w_buf[...], preferred_element_type=F32)
    length = jnp.sum(head * head, axis=-1, keepdims=True)
    emb[...] = (head * lax.rsqrt(length + 1e-06)).astype(BF)
    pl.semaphore_wait(barrier, 8)

    def x_copies():
        res = []
        for half in (0, 1):
            for k, (peer, q) in enumerate(((xp, 0), (xm, 1), (x2, 1))):
                dst = img.at[rows(i_row(0, q, half))]
                res.append(move(emb.at[rows(half * 64)], dst, sx.at[k, half], rx.at[q, half], peer))
        return res

    def x_wait(q, half):
        dst = img.at[rows(i_row(0, q, half))]
        move(emb.at[rows(half * 64)], dst, sx.at[0, half], rx.at[q, half], xp).wait_recv()

    def tx_copy(k):
        return move(emb.at[rows(k * 32, 32)], txt.at[rows(t_row(0, k), 32)], stx.at[k], rtx.at[k], xm)

    def y_copy(d, q, half, dist):
        sign = 1 - 2 * d
        idx = q * 2 + half if dist == 1 else 4 + q
        src_rel = 0 if dist == 1 else -sign
        dst_rel = -sign if dist == 1 else 2
        return move(
            img.at[rows(i_row(src_rel, q, half))], img.at[rows(i_row(dst_rel, q, half))],
            sy.at[d, idx], ry.at[d, idx], yd[d],
        )

    def z_rel(d, dist):
        rel = -dist if d == 0 else dist
        return 4 if rel == -4 else rel

    def z_copy(d, i):
        k, dist = Z_OUT[d][i]
        src = txt.at[rows(t_row(z_rel(d, dist - 1), k), 32)]
        dst = txt.at[rows(t_row(z_rel(d, dist), k), 32)]
        return move(src, dst, sz.at[d, i], rz.at[d, i], zd[d])

    S_LIST = [(0, 0), (0, 1)] + [
        (z_rel(d, Z_OUT[d][i][1]), Z_OUT[d][i][0] // 2) for i in range(0, 14, 2) for d in (0, 1)
    ]

    def s_copy(n):
        rel, half = S_LIST[n]
        part = txt.at[rows(t_row(rel, half * 2))]
        return move(part, part, ss.at[n], rs.at[n], sib)

    @pl.when(is_img)
    def _():
        for copy in x_copies():
            copy.start()
        img[256:384, :] = emb[...]

    @pl.when(jnp.logical_and(is_txt, guest))
    def _():
        for k in range(4):
            tx_copy(k).start()

    @pl.when(jnp.logical_and(is_txt, home))
    def _():
        txt[896:1024, :] = emb[...]
        for k in range(4):
            for d in (0, 1):
                z_copy(d, k).start()
        for n in (0, 1):
            s_copy(n).start()

    def y_pair(q, half):
        for d in (0, 1):
            y_copy(d, q, half, 1).start()

    @pl.when(is_img)
    def _():
        y_pair(0, 0)
        y_pair(0, 1)

    fetches[3].wait()
    for rel, slot in Z_SLOT.items():
        row = ((lax.rem(z + rel + 8, 8) * 4 + y) * 2 + h) * 2 + t
        txt_ids[:, slot * 128 : slot * 128 + 128] = jnp.broadcast_to(ids[pl.ds(row, 1), :], (8, 128))
    for (rel, q), slot in I_SLOT.items():
        row = ((z * 4 + lax.rem(y + rel + 4, 4)) * 2 + lax.rem(h + q, 2)) * 2 + c
        block = jnp.broadcast_to(ids[pl.ds(row, 1), :], (128, 128))
        img_ids[slot * 128 : slot * 128 + 128, :] = block.T

    @pl.when(jnp.logical_and(is_img, home))
    def _():
        for k in range(4):
            tx_copy(k).wait_recv()
            for d in (0, 1):
                z_copy(d, k).start()
        for n in (0, 1):
            s_copy(n).start()

    def z_steps(*steps):
        @pl.when(home)
        def _():
            for i in steps:
                for d in (0, 1):
                    z_copy(d, i).wait_recv()
                    k, dist = Z_OUT[d][i]
                    if (k, dist + 1) in Z_OUT[d]:
                        z_copy(d, Z_OUT[d].index((k, dist + 1))).start()
                    if i % 2:
                        s_copy(2 + i // 2 * 2 + d).start()

    def y_relay(q):
        for d in (0, 1):
            y_copy(d, q, d, 1).wait_recv()
            y_copy(d, q, d, 2).start()

    def xw_copy(q, half):
        return move(
            img.at[rows(i_row(2, 0, half))], img.at[rows(i_row(2, q, half))], sxw.at[q, half], rxw.at[q, half],
            (xp, xm)[q],
        )

    @pl.when(is_img)
    def _():
        y_relay(0)
        z_steps(0, 1, 2, 3)
        x_wait(1, 0)
        y_copy(0, 1, 0, 1).start()
        x_wait(1, 1)
        y_copy(1, 1, 1, 1).start()
        for d in (0, 1):
            y_copy(d, 0, d, 2).wait_recv()
            for q in (0, 1):
                xw_copy(q, d).start()
        z_steps(4, 5, 6, 7)
        y_relay(1)
        for d in (0, 1):
            y_copy(d, 1, 1 - d, 1).start()

    @pl.when(is_txt)
    def _():
        z_steps(0, 1, 2, 3)
        for q in (0, 1):
            x_wait(q, 0)
            y_pair(q, 0)
        z_steps(4, 5, 6, 7)
        for q in (0, 1):
            x_wait(q, 1)
            y_pair(q, 1)

    z_steps(*range(8, 14))

    def y_need(q):
        for d in (0, 1):
            y_copy(d, q, 1 - d, 1).wait_recv()

            @pl.when(is_txt)
            def _():
                y_copy(d, q, d, 1).wait_recv()

    def far_need():
        @pl.when(is_img)
        def _():
            for d in (0, 1):
                y_copy(d, 1, d, 2).wait_recv()

        @pl.when(is_txt)
        def _():
            for q in (0, 1):
                for half in (0, 1):
                    xw_copy(q, half).wait_recv()

    @pl.when(guest)
    def _():
        for n in range(16):
            s_copy(n).wait_recv()

    scale = jnp.exp(jnp.full((1, 1), log_scale[0], F32))
    shift = bias[0]

    def tile(slot):
        part = pl.ds(slot * 256, 256)
        logits = scale * lax.dot_general(
            img[part, :], txt[...], (((1,), (1,)), ((), ())), preferred_element_type=F32
        ) + shift
        same = img_ids[part, 0:1] == txt_ids[0:1, :]
        weight_ = 1.0 / (1.0 + jnp.exp(jnp.minimum(jnp.where(same, logits, -logits), 88.0)))
        coef[part, :] = jnp.where(same, -weight_, weight_).astype(BF)
        g_img[part, :] = jnp.dot(coef[part, :], txt[...], preferred_element_type=F32)

    def yr_copy(d, q, half, dist):
        sign = 1 - 2 * d
        if dist == 2:
            return move(
                s_img.at[rows(i_row(2, q, half))], r_y2.at[rows((d * 2 + q) * 64)],
                syr.at[d, 4 + q], ryr.at[d, 4 + q], yd[d],
            )
        idx = q * 2 + half
        return move(
            s_img.at[rows(i_row(sign, q, half))], r_y1.at[rows((d * 4 + idx) * 64)],
            syr.at[d, idx], ryr.at[d, idx], yd[d],
        )

    def y_send(q, merged):
        for d in (0, 1):
            sign = 1 - 2 * d
            half = d if merged else 1 - d
            start = i_row(sign, q, half)
            total = g_img[start : start + 64, :]
            if merged:
                yr_copy(d, q, d, 2).wait_recv()
                total = total + r_y2[(d * 2 + q) * 64 : (d * 2 + q) * 64 + 64, :].astype(F32)
            s_img[start : start + 64, :] = total.astype(BF)
            yr_copy(d, q, half, 1).start()

    y_need(0)
    tile(2)
    y_send(0, False)
    far_need()
    tile(0)
    s_img[0:256, :] = g_img[0:256, :].astype(BF)
    for q in (0, 1):
        for d in (0, 1):
            yr_copy(d, q, d, 2).start()
    y_need(1)
    tile(3)
    y_send(1, False)
    tile(1)

    def s2_copy(u):
        part = pl.ds(*UNITS[u])
        return move(s_txt.at[part], r_sib.at[part], ss2.at[u], rs2.at[u], sib)

    def text_dot(start, n):
        return lax.dot_general(
            coef[:, start : start + n], img[...], (((0,), (0,)), ((), ())), preferred_element_type=F32
        )

    def text_unit(u):
        start, n = UNITS[u]
        g_txt[start : start + n, :] = text_dot(start, n)

        @pl.when(guest)
        def _():
            s_txt[start : start + n, :] = g_txt[start : start + n, :].astype(BF)
            s2_copy(u).start()

    def back(d, i):
        k, dist = Z_BACK[i]
        rel = dist if d == 0 or dist == 4 else -dist
        return t_row(rel, k ^ (2 * d))

    def zr_copy(d, i):
        return move(
            s_txt.at[rows(back(d, i), 32)], r_z.at[rows((d * 14 + i) * 32, 32)], szr.at[d, i], rzr.at[d, i], zd[d]
        )

    def zr_take(d, i):
        zr_copy(d, i).wait_recv()
        return r_z[(d * 14 + i) * 32 : (d * 14 + i) * 32 + 32, :].astype(F32)

    def zr_steps(*steps):
        @pl.when(home)
        def _():
            for i in steps:
                for d in (0, 1):
                    start = back(d, i)
                    total = g_txt[start : start + 32, :] + r_sib[start : start + 32, :].astype(F32)
                    if i >= 4:
                        total = total + zr_take(d, i - 4)
                    s_txt[start : start + 32, :] = total.astype(BF)
                    zr_copy(d, i).start()

    def xr_copies(q, half):
        src = s_x.at[rows(q * 128 + half * 64)]
        if q == 0:
            return [(is_txt, move(src, r_x.at[rows(half * 64)], sxr.at[q, half], rxr.at[0, half], xm))]
        return [
            (is_txt, move(src, r_x.at[rows(128 + half * 64)], sxr.at[q, half], rxr.at[1, half], xp)),
            (is_img, move(src, r_x.at[rows(256 + half * 64)], sxr.at[q, half], rxr.at[2, half], x2)),
        ]

    def y_final(q, half):
        for d in (0, 1):
            yr_copy(d, q, half, 1).wait_recv()
        start = i_row(0, q, half)
        k = (q * 2 + half) * 64
        total = g_img[start : start + 64, :] + r_y1[k : k + 64, :].astype(F32) + r_y1[256 + k : 256 + k + 64, :].astype(F32)
        if q == 0:
            g_img[start : start + 64, :] = total
        s_x[q * 128 + half * 64 : q * 128 + half * 64 + 64, :] = total.astype(BF)
        for cond, copy in xr_copies(q, half):
            pl.when(cond)(copy.start)

    def s2_wait(*units):
        @pl.when(home)
        def _():
            for u in units:
                s2_copy(u).wait_recv()

    text_unit(0)
    y_send(0, True)
    y_send(1, True)
    s2_wait(0)
    zr_steps(0, 1, 2, 3)
    text_unit(1)
    text_unit(2)
    s2_wait(1, 2)
    zr_steps(4, 5, 6, 7)
    y_final(0, 0)
    y_final(0, 1)
    zr_steps(8, 9)
    y_final(1, 0)
    zr_steps(10, 11)
    y_final(1, 1)
    zr_steps(12, 13)

    def f_copy(k):
        return move(s_txt.at[rows(t_row(0, k), 32)], r_fin.at[rows(k * 32, 32)], sf.at[k], rf.at[k], xp)

    @pl.when(home)
    def _():
        for k in (2, 3, 0, 1):
            start = t_row(0, k)
            total = g_txt[start : start + 32, :] + r_sib[start : start + 32, :].astype(F32)
            for d in (0, 1):
                total = total + zr_take(d, 10 + ((2, 3, 0, 1).index(k ^ (2 * d))))

            @pl.when(is_txt)
            def _():
                out[0, k * 32 : k * 32 + 32, :] = total

            @pl.when(is_img)
            def _():
                s_txt[start : start + 32, :] = total.astype(BF)
                f_copy(k).start()

    @pl.when(is_img)
    def _():
        for half in (0, 1):
            for k in range(3):
                part = r_x.at[rows(k * 128 + half * 64)]
                move(part, part, sxr.at[0, half], rxr.at[k, half], xp).wait_recv()
            total = g_img[i_row(0, 0, half) : i_row(0, 0, half) + 64, :]
            for k in range(3):
                total = total + r_x[k * 128 + half * 64 : k * 128 + half * 64 + 64, :].astype(F32)
            out[0, half * 64 : half * 64 + 64, :] = total

    @pl.when(jnp.logical_and(is_txt, guest))
    def _():
        for k in (2, 3, 0, 1):
            f_copy(k).wait_recv()
            out[0, k * 32 : k * 32 + 32, :] = r_fin[k * 32 : k * 32 + 32, :].astype(F32)

    @pl.when(is_img)
    def _():
        for copy in x_copies():
            copy.wait_send()
        for q in (0, 1):
            for d in (0, 1):
                y_copy(d, q, d, 2).wait_send()
                xw_copy(q, d).wait_send()

    @pl.when(jnp.logical_and(is_txt, guest))
    def _():
        for k in range(4):
            tx_copy(k).wait_send()

    for d in (0, 1):
        for q in (0, 1):
            for half in (0, 1):
                y_copy(d, q, half, 1).wait_send()
                yr_copy(d, q, half, 1).wait_send()
            yr_copy(d, q, d, 2).wait_send()

    @pl.when(home)
    def _():
        for i in range(14):
            for d in (0, 1):
                z_copy(d, i).wait_send()
                zr_copy(d, i).wait_send()
        for n in range(16):
            s_copy(n).wait_send()

    @pl.when(guest)
    def _():
        for u in range(3):
            s2_copy(u).wait_send()

    for q in (0, 1):
        for half in (0, 1):
            for cond, copy in xr_copies(q, half):
                pl.when(cond)(copy.wait_send)

    @pl.when(jnp.logical_and(is_img, home))
    def _():
        for k in range(4):
            f_copy(k).wait_send()


def on_device(pooled, final_gain, head_weight, pair_ids, log_scale, bias):
    n, d = pooled.shape[1:]
    hbm = pl.BlockSpec(memory_space=pl.ANY)
    smem = pl.BlockSpec(memory_space=pltpu.SMEM)
    buf = lambda r, kind=BF: pltpu.VMEM((r, d), kind)
    dma = pltpu.SemaphoreType.DMA
    return pl.pallas_call(
        kernel,
        out_shape=jax.ShapeDtypeStruct((1, n, d), F32),
        in_specs=[hbm, hbm, hbm, hbm, smem, smem],
        out_specs=pl.BlockSpec(memory_space=pltpu.VMEM),
        scratch_shapes=[
            buf(n), buf(1, F32), pltpu.VMEM((128, 128), jnp.int32), buf(d), buf(128), buf(1024), buf(1024), pltpu.VMEM((1024, 1024), BF), buf(1024, F32), buf(1024, F32),
            buf(1024), buf(256), buf(1024), buf(1024), buf(14 * 64), buf(4 * 64), buf(8 * 64), buf(6 * 64), buf(128),
            pltpu.VMEM((1024, 128), jnp.int32), pltpu.VMEM((8, 1024), jnp.int32),
            dma((4,)), dma((3, 2)), dma((2, 2)), dma((2, 2)), dma((2, 2)), dma((4,)), dma((4,)), dma((2, 6)), dma((2, 6)), dma((2, 14)), dma((2, 14)),
            dma((16,)), dma((16,)), dma((3,)), dma((3,)), dma((2, 14)), dma((2, 14)), dma((2, 6)), dma((2, 6)),
            dma((2, 2)), dma((3, 2)), dma((4,)), dma((4,)),
        ],
        compiler_params=pltpu.CompilerParams(collective_id=0, has_side_effects=True, vmem_limit_bytes=60 * 2**20),
        name="towers",
    )(pooled, final_gain, head_weight, pair_ids.reshape(128, 128), log_scale, bias)


def solution(mesh):
    placed = (P("tower", "blk", None), P("tower", None), P("tower", None, None), P(), P(), P())
    return jax.shard_map(
        on_device, mesh=mesh, in_specs=placed, out_specs=P("tower", "blk", None), check_vma=False
    )
```

```python
import jax
import jax.numpy as jnp
from jax import lax
from jax.experimental import pallas as pl
from jax.experimental.pallas import tpu as pltpu
from jax.sharding import PartitionSpec as P

MESH = pl.DeviceIdType.MESH
BF = jnp.bfloat16
F32 = jnp.float32

I_SLOT = {(2, 0): 0, (2, 1): 1, (0, 0): 2, (0, 1): 3, (1, 0): 4, (-1, 0): 5, (1, 1): 6, (-1, 1): 7}
Z_SLOT = {4: 0, 3: 1, -3: 2, 2: 3, -2: 4, 1: 5, -1: 6, 0: 7}
UNITS = ((0, 384), (384, 256), (640, 384))
Z_OUT = tuple([(k, dist) for dist in (1, 2, 3) for k in range(4)] + [(k + 2 * d, 4) for k in (0, 1)] for d in (0, 1))
Z_BACK = ((0, 4), (1, 4)) + tuple((k, dist) for dist in (3, 2, 1) for k in (2, 3, 0, 1))


def kernel(
    pooled_hbm, gain_hbm, weight, ids_hbm, log_scale, bias, out,
    pooled, gain, ids, w_buf, emb, img, txt, coef, g_img, g_txt, s_img, s_x, s_txt, r_sib, r_z, r_y2, r_y1, r_x, r_fin,
    img_ids, txt_ids,
    in_sem, sx, rx, sxw, rxw, stx, rtx, sy, ry, sz, rz, ss, rs, ss2, rs2, szr, rzr, syr, ryr, sxr, rxr, sf, rf,
):
    t = lax.axis_index("tower")
    b = lax.axis_index("blk")
    c = lax.rem(b, 2)
    h = lax.rem(b // 2, 2)
    y = lax.rem(b // 4, 4)
    z = b // 16
    x = h * 2 + t
    is_img = t == 0
    is_txt = t == 1
    home = c == t
    guest = c != t

    def at(dx=0, dy=0, dz=0, dc=0):
        nx = lax.rem(x + dx + 4, 4)
        ny = lax.rem(y + dy + 4, 4)
        nz = lax.rem(z + dz + 8, 8)
        nc = lax.rem(c + dc, 2)
        return (lax.rem(nx, 2), ((nz * 4 + ny) * 2 + nx // 2) * 2 + nc)

    xp, xm, x2 = at(dx=1), at(dx=-1), at(dx=2)
    yd = (at(dy=1), at(dy=-1))
    zd = (at(dz=1), at(dz=-1))
    sib = at(dc=1)

    fetches = [
        pltpu.make_async_copy(a, b, in_sem.at[n])
        for n, (a, b) in enumerate(
            ((pooled_hbm.at[0], pooled), (gain_hbm, gain), (weight.at[0], w_buf), (ids_hbm, ids))
        )
    ]
    for fetch in fetches:
        fetch.start()

    barrier = pltpu.get_barrier_semaphore()
    for peer in (xp, xm, x2, yd[0], yd[1], zd[0], zd[1], sib):
        pl.semaphore_signal(barrier, 1, device_id=peer, device_id_type=MESH)

    def move(src, dst, send, recv, peer):
        return pltpu.make_async_remote_copy(
            src_ref=src, dst_ref=dst, send_sem=send, recv_sem=recv, device_id=peer, device_id_type=MESH
        )

    def rows(start, n=64):
        return pl.ds(start, n)

    def i_row(rel, q, half):
        return I_SLOT[rel, q] * 128 + half * 64

    def t_row(rel, k):
        return Z_SLOT[rel] * 128 + k * 32

    fetches[0].wait()
    fetches[1].wait()
    values = pooled[...].astype(F32)
    center = values - jnp.mean(values, axis=-1, keepdims=True)
    spread = jnp.mean(center * center, axis=-1, keepdims=True)
    normed = (center * lax.rsqrt(spread + 1e-06) * gain[...]).astype(BF)
    fetches[2].wait()
    head = jnp.dot(normed, w_buf[...], preferred_element_type=F32)
    length = jnp.sum(head * head, axis=-1, keepdims=True)
    emb[...] = (head * lax.rsqrt(length + 1e-06)).astype(BF)
    pl.semaphore_wait(barrier, 8)

    def x_copies():
        res = []
        for half in (0, 1):
            for k, (peer, q) in enumerate(((x2, 1), (xp, 0), (xm, 1))):
                dst = img.at[rows(i_row(0, q, half))]
                res.append(move(emb.at[rows(half * 64)], dst, sx.at[k, half], rx.at[q, half], peer))
        return res

    def x_wait(q, half):
        dst = img.at[rows(i_row(0, q, half))]
        move(emb.at[rows(half * 64)], dst, sx.at[0, half], rx.at[q, half], xp).wait_recv()

    def tx_copy(k):
        return move(emb.at[rows(k * 32, 32)], txt.at[rows(t_row(0, k), 32)], stx.at[k], rtx.at[k], xm)

    def y_copy(d, q, half, dist):
        sign = 1 - 2 * d
        idx = q * 2 + half if dist == 1 else 4 + q
        src_rel = 0 if dist == 1 else -sign
        dst_rel = -sign if dist == 1 else 2
        return move(
            img.at[rows(i_row(src_rel, q, half))], img.at[rows(i_row(dst_rel, q, half))],
            sy.at[d, idx], ry.at[d, idx], yd[d],
        )

    def z_rel(d, dist):
        rel = -dist if d == 0 else dist
        return 4 if rel == -4 else rel

    def z_copy(d, i):
        k, dist = Z_OUT[d][i]
        src = txt.at[rows(t_row(z_rel(d, dist - 1), k), 32)]
        dst = txt.at[rows(t_row(z_rel(d, dist), k), 32)]
        return move(src, dst, sz.at[d, i], rz.at[d, i], zd[d])

    S_LIST = [(0, 0), (0, 1)] + [
        (z_rel(d, Z_OUT[d][i][1]), Z_OUT[d][i][0] // 2) for i in range(0, 14, 2) for d in (0, 1)
    ]

    def s_copy(n):
        rel, half = S_LIST[n]
        part = txt.at[rows(t_row(rel, half * 2))]
        return move(part, part, ss.at[n], rs.at[n], sib)

    @pl.when(is_img)
    def _():
        for copy in x_copies():
            copy.start()
        img[256:384, :] = emb[...]

    @pl.when(jnp.logical_and(is_txt, guest))
    def _():
        for k in range(4):
            tx_copy(k).start()

    @pl.when(jnp.logical_and(is_txt, home))
    def _():
        txt[896:1024, :] = emb[...]
        for k in range(4):
            for d in (0, 1):
                z_copy(d, k).start()
        for n in (0, 1):
            s_copy(n).start()

    def y_pair(q, half):
        for d in (0, 1):
            y_copy(d, q, half, 1).start()

    @pl.when(is_img)
    def _():
        y_pair(0, 0)
        y_pair(0, 1)

    fetches[3].wait()
    for rel, slot in Z_SLOT.items():
        row = ((lax.rem(z + rel + 8, 8) * 4 + y) * 2 + h) * 2 + t
        txt_ids[:, slot * 128 : slot * 128 + 128] = jnp.broadcast_to(ids[pl.ds(row, 1), :], (8, 128))
    for (rel, q), slot in I_SLOT.items():
        row = ((z * 4 + lax.rem(y + rel + 4, 4)) * 2 + lax.rem(h + q, 2)) * 2 + c
        block = jnp.broadcast_to(ids[pl.ds(row, 1), :], (128, 128))
        img_ids[slot * 128 : slot * 128 + 128, :] = block.T

    @pl.when(jnp.logical_and(is_img, home))
    def _():
        for k in range(4):
            tx_copy(k).wait_recv()
            for d in (0, 1):
                z_copy(d, k).start()
        for n in (0, 1):
            s_copy(n).start()

    def z_steps(*steps):
        @pl.when(home)
        def _():
            for i in steps:
                for d in (0, 1):
                    z_copy(d, i).wait_recv()
                    k, dist = Z_OUT[d][i]
                    if (k, dist + 1) in Z_OUT[d]:
                        z_copy(d, Z_OUT[d].index((k, dist + 1))).start()
                    if i % 2:
                        s_copy(2 + i // 2 * 2 + d).start()

    def y_relay(q):
        for d in (0, 1):
            y_copy(d, q, d, 1).wait_recv()
            y_copy(d, q, d, 2).start()

    def xw_copy(q, half):
        return move(
            img.at[rows(i_row(2, 0, half))], img.at[rows(i_row(2, q, half))], sxw.at[q, half], rxw.at[q, half],
            (xp, xm)[q],
        )

    @pl.when(is_img)
    def _():
        y_relay(0)
        x_wait(1, 0)
        y_copy(0, 1, 0, 1).start()
        z_steps(0, 1, 2, 3)
        x_wait(1, 1)
        y_copy(1, 1, 1, 1).start()
        z_steps(4, 5, 6, 7)
        for d in (0, 1):
            y_copy(d, 0, d, 2).wait_recv()
            for q in (0, 1):
                xw_copy(q, d).start()
        y_relay(1)
        for d in (0, 1):
            y_copy(d, 1, 1 - d, 1).start()
        z_steps(8, 9)

    @pl.when(is_txt)
    def _():
        z_steps(0, 1, 2, 3)
        for q in (0, 1):
            x_wait(q, 0)
            y_pair(q, 0)
        z_steps(4, 5, 6, 7, 8, 9)
        for q in (0, 1):
            x_wait(q, 1)
            y_pair(q, 1)

    z_steps(10, 11)

    def guest_need(*numbers):
        @pl.when(guest)
        def _():
            for n in numbers:
                s_copy(n).wait_recv()

    def y_need(q):
        for d in (0, 1):
            y_copy(d, q, 1 - d, 1).wait_recv()

            @pl.when(is_txt)
            def _():
                y_copy(d, q, d, 1).wait_recv()

    def far_need():
        @pl.when(is_img)
        def _():
            for d in (0, 1):
                y_copy(d, 1, d, 2).wait_recv()

        @pl.when(is_txt)
        def _():
            for q in (0, 1):
                for half in (0, 1):
                    xw_copy(q, half).wait_recv()

    scale = jnp.exp(jnp.full((1, 1), log_scale[0], F32))
    shift = bias[0]

    def tile(slot, start=0, n=1024):
        part = pl.ds(slot * 256, 256)
        cols = pl.ds(start, n)
        logits = scale * lax.dot_general(
            img[part, :], txt[cols, :], (((1,), (1,)), ((), ())), preferred_element_type=F32
        ) + shift
        same = img_ids[part, 0:1] == txt_ids[0:1, cols]
        weight_ = 1.0 / (1.0 + jnp.exp(jnp.minimum(jnp.where(same, logits, -logits), 88.0)))
        coef[part, cols] = jnp.where(same, -weight_, weight_).astype(BF)
        total = jnp.dot(coef[part, cols], txt[cols, :], preferred_element_type=F32)
        if start + n < 1024 or n == 1024:
            g_img[part, :] = total + g_img[part, :] if n < 1024 else total
        else:
            g_img[part, :] = total

    def yr_copy(d, q, half, dist):
        sign = 1 - 2 * d
        if dist == 2:
            return move(
                s_img.at[rows(i_row(2, q, half))], r_y2.at[rows((d * 2 + q) * 64)],
                syr.at[d, 4 + q], ryr.at[d, 4 + q], yd[d],
            )
        idx = q * 2 + half
        return move(
            s_img.at[rows(i_row(sign, q, half))], r_y1.at[rows((d * 4 + idx) * 64)],
            syr.at[d, idx], ryr.at[d, idx], yd[d],
        )

    def y_send(q, merged):
        for d in (0, 1):
            sign = 1 - 2 * d
            half = d if merged else 1 - d
            start = i_row(sign, q, half)
            total = g_img[start : start + 64, :]
            if merged:
                yr_copy(d, q, d, 2).wait_recv()
                total = total + r_y2[(d * 2 + q) * 64 : (d * 2 + q) * 64 + 64, :].astype(F32)
            s_img[start : start + 64, :] = total.astype(BF)
            yr_copy(d, q, half, 1).start()

    guest_need(*range(11), 12)
    y_need(0)
    tile(2, 256, 768)
    tile(1, 256, 768)
    z_steps(12, 13)
    guest_need(11, 13, 14, 15)
    tile(2, 0, 256)
    y_send(0, False)
    far_need()
    tile(0)
    s_img[0:256, :] = g_img[0:256, :].astype(BF)
    for q in (0, 1):
        for d in (0, 1):
            yr_copy(d, q, d, 2).start()
    y_need(1)
    tile(3)
    y_send(1, False)
    tile(1, 0, 256)

    def s2_copy(u):
        part = pl.ds(*UNITS[u])
        return move(s_txt.at[part], r_sib.at[part], ss2.at[u], rs2.at[u], sib)

    def text_dot(start, n):
        return lax.dot_general(
            coef[:, start : start + n], img[...], (((0,), (0,)), ((), ())), preferred_element_type=F32
        )

    def text_unit(u):
        start, n = UNITS[u]
        g_txt[start : start + n, :] = text_dot(start, n)

        @pl.when(guest)
        def _():
            s_txt[start : start + n, :] = g_txt[start : start + n, :].astype(BF)
            s2_copy(u).start()

    def back(d, i):
        k, dist = Z_BACK[i]
        rel = dist if d == 0 or dist == 4 else -dist
        return t_row(rel, k ^ (2 * d))

    def zr_copy(d, i):
        return move(
            s_txt.at[rows(back(d, i), 32)], r_z.at[rows((d * 14 + i) * 32, 32)], szr.at[d, i], rzr.at[d, i], zd[d]
        )

    def zr_take(d, i):
        zr_copy(d, i).wait_recv()
        return r_z[(d * 14 + i) * 32 : (d * 14 + i) * 32 + 32, :].astype(F32)

    def zr_steps(*steps):
        @pl.when(home)
        def _():
            for i in steps:
                for d in (0, 1):
                    start = back(d, i)
                    total = g_txt[start : start + 32, :] + r_sib[start : start + 32, :].astype(F32)
                    if i >= 4:
                        total = total + zr_take(d, i - 4)
                    s_txt[start : start + 32, :] = total.astype(BF)
                    zr_copy(d, i).start()

    def xr_copies(q, half):
        src = s_x.at[rows(q * 128 + half * 64)]
        if q == 0:
            return [(is_txt, move(src, r_x.at[rows(half * 64)], sxr.at[q, half], rxr.at[0, half], xm))]
        return [
            (is_txt, move(src, r_x.at[rows(128 + half * 64)], sxr.at[q, half], rxr.at[1, half], xp)),
            (is_img, move(src, r_x.at[rows(256 + half * 64)], sxr.at[q, half], rxr.at[2, half], x2)),
        ]

    def y_final(q, half):
        for d in (0, 1):
            yr_copy(d, q, half, 1).wait_recv()
        start = i_row(0, q, half)
        k = (q * 2 + half) * 64
        total = g_img[start : start + 64, :] + r_y1[k : k + 64, :].astype(F32) + r_y1[256 + k : 256 + k + 64, :].astype(F32)
        if q == 0:
            g_img[start : start + 64, :] = total
        s_x[q * 128 + half * 64 : q * 128 + half * 64 + 64, :] = total.astype(BF)
        for cond, copy in xr_copies(q, half):
            pl.when(cond)(copy.start)

    def s2_wait(*units):
        @pl.when(home)
        def _():
            for u in units:
                s2_copy(u).wait_recv()

    text_unit(0)
    s2_wait(0)
    zr_steps(0, 1, 2, 3)
    y_send(0, True)
    text_unit(1)
    text_unit(2)
    y_send(1, True)
    s2_wait(1, 2)
    zr_steps(*range(4, 12))
    y_final(0, 0)
    y_final(0, 1)
    zr_steps(12, 13)
    y_final(1, 0)
    y_final(1, 1)

    def f_copy(k):
        return move(s_txt.at[rows(t_row(0, k), 32)], r_fin.at[rows(k * 32, 32)], sf.at[k], rf.at[k], xp)

    @pl.when(home)
    def _():
        for k in (2, 3, 0, 1):
            start = t_row(0, k)
            total = g_txt[start : start + 32, :] + r_sib[start : start + 32, :].astype(F32)
            for d in (0, 1):
                total = total + zr_take(d, 10 + ((2, 3, 0, 1).index(k ^ (2 * d))))

            @pl.when(is_txt)
            def _():
                out[0, k * 32 : k * 32 + 32, :] = total

            @pl.when(is_img)
            def _():
                s_txt[start : start + 32, :] = total.astype(BF)
                f_copy(k).start()

    @pl.when(is_img)
    def _():
        for half in (0, 1):
            for k in range(3):
                part = r_x.at[rows(k * 128 + half * 64)]
                move(part, part, sxr.at[0, half], rxr.at[k, half], xp).wait_recv()
            total = g_img[i_row(0, 0, half) : i_row(0, 0, half) + 64, :]
            for k in range(3):
                total = total + r_x[k * 128 + half * 64 : k * 128 + half * 64 + 64, :].astype(F32)
            out[0, half * 64 : half * 64 + 64, :] = total

    @pl.when(jnp.logical_and(is_txt, guest))
    def _():
        for k in (2, 3, 0, 1):
            f_copy(k).wait_recv()
            out[0, k * 32 : k * 32 + 32, :] = r_fin[k * 32 : k * 32 + 32, :].astype(F32)

    @pl.when(is_img)
    def _():
        for copy in x_copies():
            copy.wait_send()
        for q in (0, 1):
            for d in (0, 1):
                y_copy(d, q, d, 2).wait_send()
                xw_copy(q, d).wait_send()

    @pl.when(jnp.logical_and(is_txt, guest))
    def _():
        for k in range(4):
            tx_copy(k).wait_send()

    for d in (0, 1):
        for q in (0, 1):
            for half in (0, 1):
                y_copy(d, q, half, 1).wait_send()
                yr_copy(d, q, half, 1).wait_send()
            yr_copy(d, q, d, 2).wait_send()

    @pl.when(home)
    def _():
        for i in range(14):
            for d in (0, 1):
                z_copy(d, i).wait_send()
                zr_copy(d, i).wait_send()
        for n in range(16):
            s_copy(n).wait_send()

    @pl.when(guest)
    def _():
        for u in range(3):
            s2_copy(u).wait_send()

    for q in (0, 1):
        for half in (0, 1):
            for cond, copy in xr_copies(q, half):
                pl.when(cond)(copy.wait_send)

    @pl.when(jnp.logical_and(is_img, home))
    def _():
        for k in range(4):
            f_copy(k).wait_send()


def on_device(pooled, final_gain, head_weight, pair_ids, log_scale, bias):
    n, d = pooled.shape[1:]
    hbm = pl.BlockSpec(memory_space=pl.ANY)
    smem = pl.BlockSpec(memory_space=pltpu.SMEM)
    buf = lambda r, kind=BF: pltpu.VMEM((r, d), kind)
    dma = pltpu.SemaphoreType.DMA
    return pl.pallas_call(
        kernel,
        out_shape=pltpu.VMEM((1, n, d), F32),
        in_specs=[hbm, hbm, hbm, hbm, smem, smem],
        out_specs=pl.BlockSpec(memory_space=pltpu.VMEM),
        scratch_shapes=[
            buf(n), buf(1, F32), pltpu.VMEM((128, 128), jnp.int32), buf(d), buf(128), buf(1024), buf(1024), pltpu.VMEM((1024, 1024), BF), buf(1024, F32), buf(1024, F32),
            buf(1024), buf(256), buf(1024), buf(1024), buf(14 * 64), buf(4 * 64), buf(8 * 64), buf(6 * 64), buf(128),
            pltpu.VMEM((1024, 128), jnp.int32), pltpu.VMEM((8, 1024), jnp.int32),
            dma((4,)), dma((3, 2)), dma((2, 2)), dma((2, 2)), dma((2, 2)), dma((4,)), dma((4,)), dma((2, 6)), dma((2, 6)), dma((2, 14)), dma((2, 14)),
            dma((16,)), dma((16,)), dma((3,)), dma((3,)), dma((2, 14)), dma((2, 14)), dma((2, 6)), dma((2, 6)),
            dma((2, 2)), dma((3, 2)), dma((4,)), dma((4,)),
        ],
        compiler_params=pltpu.CompilerParams(collective_id=0, has_side_effects=True, vmem_limit_bytes=67043328 - 600000),
        name="towers",
    )(pooled, final_gain, head_weight, pair_ids.reshape(128, 128), log_scale, bias)


def solution(mesh):
    placed = (P("tower", "blk", None), P("tower", None), P("tower", None, None), P(), P(), P())
    return jax.shard_map(
        on_device, mesh=mesh, in_specs=placed, out_specs=P("tower", "blk", None), check_vma=False
    )
```

```python
import jax
import jax.numpy as jnp
from jax import lax
from jax.experimental import pallas as pl
from jax.experimental.pallas import tpu as pltpu
from jax.sharding import PartitionSpec as P

MESH = pl.DeviceIdType.MESH
BF = jnp.bfloat16
F32 = jnp.float32

I_SLOT = {(2, 0): 0, (2, 1): 1, (0, 0): 2, (0, 1): 3, (1, 0): 4, (-1, 0): 5, (1, 1): 6, (-1, 1): 7}
Z_SLOT = {4: 0, 3: 1, -3: 2, 2: 3, -2: 4, 1: 5, -1: 6, 0: 7}
UNITS = ((0, 384), (384, 256), (640, 384))
Z_OUT = tuple([(k, dist) for dist in (1, 2, 3) for k in range(4)] + [(k + 2 * d, 4) for k in (0, 1)] for d in (0, 1))
Z_BACK = ((0, 4), (1, 4)) + tuple((k, dist) for dist in (3, 2, 1) for k in (2, 3, 0, 1))


def kernel(
    pooled_hbm, gain_hbm, weight, ids_hbm, log_scale, bias, out,
    pooled, gain, ids, w_buf, emb, img, txt, coef, g_img, g_txt, s_img, s_x, s_txt, r_sib, r_z, r_y2, r_y1, r_x, r_fin,
    img_ids, txt_ids,
    in_sem, sx, rx, sxw, rxw, stx, rtx, sy, ry, sz, rz, ss, rs, ss2, rs2, szr, rzr, syr, ryr, sxr, rxr, sf, rf,
):
    t = lax.axis_index("tower")
    b = lax.axis_index("blk")
    c = lax.rem(b, 2)
    h = lax.rem(b // 2, 2)
    y = lax.rem(b // 4, 4)
    z = b // 16
    x = h * 2 + t
    is_img = t == 0
    is_txt = t == 1
    home = c == t
    guest = c != t

    def at(dx=0, dy=0, dz=0, dc=0):
        nx = lax.rem(x + dx + 4, 4)
        ny = lax.rem(y + dy + 4, 4)
        nz = lax.rem(z + dz + 8, 8)
        nc = lax.rem(c + dc, 2)
        return (lax.rem(nx, 2), ((nz * 4 + ny) * 2 + nx // 2) * 2 + nc)

    xp, xm, x2 = at(dx=1), at(dx=-1), at(dx=2)
    yd = (at(dy=1), at(dy=-1))
    zd = (at(dz=1), at(dz=-1))
    sib = at(dc=1)

    fetches = [
        pltpu.make_async_copy(a, b, in_sem.at[n])
        for n, (a, b) in enumerate(
            ((pooled_hbm.at[0], pooled), (gain_hbm, gain), (weight.at[0], w_buf), (ids_hbm, ids))
        )
    ]
    for fetch in fetches:
        fetch.start()

    barrier = pltpu.get_barrier_semaphore()
    for peer in (xp, xm, x2, yd[0], yd[1], zd[0], zd[1], sib):
        pl.semaphore_signal(barrier, 1, device_id=peer, device_id_type=MESH)

    def move(src, dst, send, recv, peer):
        return pltpu.make_async_remote_copy(
            src_ref=src, dst_ref=dst, send_sem=send, recv_sem=recv, device_id=peer, device_id_type=MESH
        )

    def rows(start, n=64):
        return pl.ds(start, n)

    def i_row(rel, q, half):
        return I_SLOT[rel, q] * 128 + half * 64

    def t_row(rel, k):
        return Z_SLOT[rel] * 128 + k * 32

    fetches[0].wait()
    fetches[1].wait()
    values = pooled[...].astype(F32)
    center = values - jnp.mean(values, axis=-1, keepdims=True)
    spread = jnp.mean(center * center, axis=-1, keepdims=True)
    normed = (center * lax.rsqrt(spread + 1e-06) * gain[...]).astype(BF)
    fetches[2].wait()
    head = jnp.dot(normed, w_buf[...], preferred_element_type=F32)
    length = jnp.sum(head * head, axis=-1, keepdims=True)
    emb[...] = (head * lax.rsqrt(length + 1e-06)).astype(BF)
    pl.semaphore_wait(barrier, 8)

    def x_copies():
        res = []
        for half in (0, 1):
            for k, (peer, q) in enumerate(((x2, 1), (xp, 0), (xm, 1))):
                dst = img.at[rows(i_row(0, q, half))]
                res.append(move(emb.at[rows(half * 64)], dst, sx.at[k, half], rx.at[q, half], peer))
        return res

    def x_wait(q, half):
        dst = img.at[rows(i_row(0, q, half))]
        move(emb.at[rows(half * 64)], dst, sx.at[0, half], rx.at[q, half], xp).wait_recv()

    def tx_copy(k):
        return move(emb.at[rows(k * 32, 32)], txt.at[rows(t_row(0, k), 32)], stx.at[k], rtx.at[k], xm)

    def y_copy(d, q, half, dist):
        sign = 1 - 2 * d
        idx = q * 2 + half if dist == 1 else 4 + q
        src_rel = 0 if dist == 1 else -sign
        dst_rel = -sign if dist == 1 else 2
        return move(
            img.at[rows(i_row(src_rel, q, half))], img.at[rows(i_row(dst_rel, q, half))],
            sy.at[d, idx], ry.at[d, idx], yd[d],
        )

    def z_rel(d, dist):
        rel = -dist if d == 0 else dist
        return 4 if rel == -4 else rel

    def z_copy(d, i):
        k, dist = Z_OUT[d][i]
        src = txt.at[rows(t_row(z_rel(d, dist - 1), k), 32)]
        dst = txt.at[rows(t_row(z_rel(d, dist), k), 32)]
        return move(src, dst, sz.at[d, i], rz.at[d, i], zd[d])

    S_LIST = [(0, 0), (0, 1)] + [
        (z_rel(d, Z_OUT[d][i][1]), Z_OUT[d][i][0] // 2) for i in range(0, 14, 2) for d in (0, 1)
    ]

    def s_copy(n):
        rel, half = S_LIST[n]
        part = txt.at[rows(t_row(rel, half * 2))]
        return move(part, part, ss.at[n], rs.at[n], sib)

    @pl.when(is_img)
    def _():
        for copy in x_copies():
            copy.start()
        img[256:384, :] = emb[...]

    @pl.when(jnp.logical_and(is_txt, guest))
    def _():
        for k in range(4):
            tx_copy(k).start()

    @pl.when(jnp.logical_and(is_txt, home))
    def _():
        txt[896:1024, :] = emb[...]
        for k in range(4):
            for d in (0, 1):
                z_copy(d, k).start()
        for n in (0, 1):
            s_copy(n).start()

    def y_pair(q, half):
        for d in (0, 1):
            y_copy(d, q, half, 1).start()

    @pl.when(is_img)
    def _():
        y_pair(0, 0)
        y_pair(0, 1)

    fetches[3].wait()
    for rel, slot in Z_SLOT.items():
        row = ((lax.rem(z + rel + 8, 8) * 4 + y) * 2 + h) * 2 + t
        txt_ids[:, slot * 128 : slot * 128 + 128] = jnp.broadcast_to(ids[pl.ds(row, 1), :], (8, 128))
    for (rel, q), slot in I_SLOT.items():
        row = ((z * 4 + lax.rem(y + rel + 4, 4)) * 2 + lax.rem(h + q, 2)) * 2 + c
        block = jnp.broadcast_to(ids[pl.ds(row, 1), :], (128, 128))
        img_ids[slot * 128 : slot * 128 + 128, :] = block.T

    @pl.when(jnp.logical_and(is_img, home))
    def _():
        for k in range(4):
            tx_copy(k).wait_recv()
            for d in (0, 1):
                z_copy(d, k).start()
        for n in (0, 1):
            s_copy(n).start()

    def z_steps(*steps):
        @pl.when(home)
        def _():
            for i in steps:
                for d in (0, 1):
                    z_copy(d, i).wait_recv()
                    k, dist = Z_OUT[d][i]
                    if (k, dist + 1) in Z_OUT[d]:
                        z_copy(d, Z_OUT[d].index((k, dist + 1))).start()
                    if i % 2:
                        s_copy(2 + i // 2 * 2 + d).start()

    def y_relay(q):
        for d in (0, 1):
            y_copy(d, q, d, 1).wait_recv()
            y_copy(d, q, d, 2).start()

    def xw_copy(q, half):
        return move(
            img.at[rows(i_row(2, 0, half))], img.at[rows(i_row(2, q, half))], sxw.at[q, half], rxw.at[q, half],
            (xp, xm)[q],
        )

    @pl.when(is_img)
    def _():
        y_relay(0)
        x_wait(1, 0)
        y_copy(0, 1, 0, 1).start()
        z_steps(0, 1, 2, 3)
        x_wait(1, 1)
        y_copy(1, 1, 1, 1).start()
        z_steps(4, 5, 6, 7)
        for d in (0, 1):
            y_copy(d, 0, d, 2).wait_recv()
            for q in (0, 1):
                xw_copy(q, d).start()
        y_relay(1)
        for d in (0, 1):
            y_copy(d, 1, 1 - d, 1).start()
        z_steps(8, 9)

    @pl.when(is_txt)
    def _():
        z_steps(0, 1, 2, 3)
        for q in (0, 1):
            x_wait(q, 0)
            y_pair(q, 0)
        z_steps(4, 5, 6, 7, 8, 9)
        for q in (0, 1):
            x_wait(q, 1)
            y_pair(q, 1)

    z_steps(10, 11)

    def guest_need(*numbers):
        @pl.when(guest)
        def _():
            for n in numbers:
                s_copy(n).wait_recv()

    def y_need(q):
        for d in (0, 1):
            y_copy(d, q, 1 - d, 1).wait_recv()

            @pl.when(is_txt)
            def _():
                y_copy(d, q, d, 1).wait_recv()

    def far_need():
        @pl.when(is_img)
        def _():
            for d in (0, 1):
                y_copy(d, 1, d, 2).wait_recv()

        @pl.when(is_txt)
        def _():
            for q in (0, 1):
                for half in (0, 1):
                    xw_copy(q, half).wait_recv()

    scale = jnp.exp(jnp.full((1, 1), log_scale[0], F32))
    shift = bias[0]

    def tile(slot, start=0, n=1024):
        part = pl.ds(slot * 256, 256)
        cols = pl.ds(start, n)
        logits = scale * lax.dot_general(
            img[part, :], txt[cols, :], (((1,), (1,)), ((), ())), preferred_element_type=F32
        ) + shift
        same = img_ids[part, 0:1] == txt_ids[0:1, cols]
        weight_ = 1.0 / (1.0 + jnp.exp(jnp.minimum(jnp.where(same, logits, -logits), 88.0)))
        coef[part, cols] = jnp.where(same, -weight_, weight_).astype(BF)
        total = jnp.dot(coef[part, cols], txt[cols, :], preferred_element_type=F32)
        if start + n < 1024 or n == 1024:
            g_img[part, :] = total + g_img[part, :] if n < 1024 else total
        else:
            g_img[part, :] = total

    def q_row(rel, q, k):
        return I_SLOT[rel, q] * 128 + k * 32

    def yr_copy(d, q, k, dist):
        sign = 1 - 2 * d
        if dist == 2:
            n = q * 2 + k - 2 * d
            return move(
                s_img.at[rows(q_row(2, q, k), 32)], r_y2.at[rows((d * 4 + n) * 32, 32)],
                syr.at[d, 8 + n], ryr.at[d, 8 + n], yd[d],
            )
        n = q * 4 + k
        return move(
            s_img.at[rows(q_row(sign, q, k), 32)], r_y1.at[rows((d * 8 + n) * 32, 32)],
            syr.at[d, n], ryr.at[d, n], yd[d],
        )

    def y_send(q, merged):
        for j in (0, 1):
            for d in (0, 1):
                sign = 1 - 2 * d
                k = 2 * (d if merged else 1 - d) + j
                start = q_row(sign, q, k)
                total = g_img[start : start + 32, :]
                if merged:
                    yr_copy(d, q, k, 2).wait_recv()
                    far = (d * 4 + q * 2 + j) * 32
                    total = total + r_y2[far : far + 32, :].astype(F32)
                s_img[start : start + 32, :] = total.astype(BF)
                yr_copy(d, q, k, 1).start()

    guest_need(*range(11), 12)
    y_need(0)
    tile(2, 256, 768)
    tile(1, 256, 768)
    z_steps(12, 13)
    guest_need(11, 13, 14, 15)
    tile(2, 0, 256)
    y_send(0, False)
    far_need()
    tile(0)
    s_img[0:256, :] = g_img[0:256, :].astype(BF)
    for q in (0, 1):
        for j in (0, 1):
            for d in (0, 1):
                yr_copy(d, q, 2 * d + j, 2).start()
    y_need(1)
    tile(3)
    y_send(1, False)
    tile(1, 0, 256)

    def s2_copy(u):
        part = pl.ds(*UNITS[u])
        return move(s_txt.at[part], r_sib.at[part], ss2.at[u], rs2.at[u], sib)

    def text_dot(start, n):
        return lax.dot_general(
            coef[:, start : start + n], img[...], (((0,), (0,)), ((), ())), preferred_element_type=F32
        )

    def text_unit(u):
        start, n = UNITS[u]
        g_txt[start : start + n, :] = text_dot(start, n)

        @pl.when(guest)
        def _():
            s_txt[start : start + n, :] = g_txt[start : start + n, :].astype(BF)
            s2_copy(u).start()

    def back(d, i):
        k, dist = Z_BACK[i]
        rel = dist if d == 0 or dist == 4 else -dist
        return t_row(rel, k ^ (2 * d))

    def zr_copy(d, i):
        return move(
            s_txt.at[rows(back(d, i), 32)], r_z.at[rows((d * 14 + i) * 32, 32)], szr.at[d, i], rzr.at[d, i], zd[d]
        )

    def zr_take(d, i):
        zr_copy(d, i).wait_recv()
        return r_z[(d * 14 + i) * 32 : (d * 14 + i) * 32 + 32, :].astype(F32)

    def zr_steps(*steps):
        @pl.when(home)
        def _():
            for i in steps:
                for d in (0, 1):
                    start = back(d, i)
                    total = g_txt[start : start + 32, :] + r_sib[start : start + 32, :].astype(F32)
                    if i >= 4:
                        total = total + zr_take(d, i - 4)
                    s_txt[start : start + 32, :] = total.astype(BF)
                    zr_copy(d, i).start()

    def xr_copies(q, k):
        src = s_x.at[rows(q * 128 + k * 32, 32)]
        if q == 0:
            return [(is_txt, move(src, r_x.at[rows(k * 32, 32)], sxr.at[q, k], rxr.at[0, k], xm))]
        return [
            (is_txt, move(src, r_x.at[rows(128 + k * 32, 32)], sxr.at[q, k], rxr.at[1, k], xp)),
            (is_img, move(src, r_x.at[rows(256 + k * 32, 32)], sxr.at[q, k], rxr.at[2, k], x2)),
        ]

    LAST = (0, 2, 1, 3)

    def y_final(q):
        for k in LAST:
            for d in (0, 1):
                yr_copy(d, q, k, 1).wait_recv()
            start = q_row(0, q, k)
            n = (q * 4 + k) * 32
            total = g_img[start : start + 32, :] + r_y1[n : n + 32, :].astype(F32) + r_y1[256 + n : 288 + n, :].astype(F32)
            if q == 0:
                g_img[start : start + 32, :] = total
            s_x[q * 128 + k * 32 : q * 128 + k * 32 + 32, :] = total.astype(BF)
            for cond, copy in xr_copies(q, k):
                pl.when(cond)(copy.start)

    def s2_wait(*units):
        @pl.when(home)
        def _():
            for u in units:
                s2_copy(u).wait_recv()

    text_unit(0)
    y_send(0, True)
    s2_wait(0)
    zr_steps(0, 1, 2, 3)
    text_unit(1)
    text_unit(2)
    y_send(1, True)
    s2_wait(1, 2)
    zr_steps(*range(4, 8))

    @pl.when(is_txt)
    def _():
        y_final(0)
        zr_steps(8, 9, 10, 11)
        y_final(1)
        zr_steps(12, 13)

    @pl.when(is_img)
    def _():
        zr_steps(8, 9, 10, 11)
        y_final(0)
        zr_steps(12, 13)
        y_final(1)

    def f_copy(k):
        return move(s_txt.at[rows(t_row(0, k), 32)], r_fin.at[rows(k * 32, 32)], sf.at[k], rf.at[k], xp)

    @pl.when(home)
    def _():
        for k in (2, 3, 0, 1):
            start = t_row(0, k)
            total = g_txt[start : start + 32, :] + r_sib[start : start + 32, :].astype(F32)
            for d in (0, 1):
                total = total + zr_take(d, 10 + ((2, 3, 0, 1).index(k ^ (2 * d))))

            @pl.when(is_txt)
            def _():
                out[0, k * 32 : k * 32 + 32, :] = total

            @pl.when(is_img)
            def _():
                s_txt[start : start + 32, :] = total.astype(BF)
                f_copy(k).start()

    @pl.when(is_img)
    def _():
        for k in LAST:
            start = q_row(0, 0, k)
            total = g_img[start : start + 32, :]
            for n in range(3):
                part = rows(n * 128 + k * 32, 32)
                move(r_x.at[part], r_x.at[part], sxr.at[0, k], rxr.at[n, k], xp).wait_recv()
                total = total + r_x[part, :].astype(F32)
            out[0, k * 32 : k * 32 + 32, :] = total

    @pl.when(jnp.logical_and(is_txt, guest))
    def _():
        for k in (2, 3, 0, 1):
            f_copy(k).wait_recv()
            out[0, k * 32 : k * 32 + 32, :] = r_fin[k * 32 : k * 32 + 32, :].astype(F32)

    @pl.when(is_img)
    def _():
        for copy in x_copies():
            copy.wait_send()
        for q in (0, 1):
            for d in (0, 1):
                y_copy(d, q, d, 2).wait_send()
                xw_copy(q, d).wait_send()

    @pl.when(jnp.logical_and(is_txt, guest))
    def _():
        for k in range(4):
            tx_copy(k).wait_send()

    for d in (0, 1):
        for q in (0, 1):
            for half in (0, 1):
                y_copy(d, q, half, 1).wait_send()
                yr_copy(d, q, 2 * d + half, 2).wait_send()
            for k in range(4):
                yr_copy(d, q, k, 1).wait_send()

    @pl.when(home)
    def _():
        for i in range(14):
            for d in (0, 1):
                z_copy(d, i).wait_send()
                zr_copy(d, i).wait_send()
        for n in range(16):
            s_copy(n).wait_send()

    @pl.when(guest)
    def _():
        for u in range(3):
            s2_copy(u).wait_send()

    for q in (0, 1):
        for k in range(4):
            for cond, copy in xr_copies(q, k):
                pl.when(cond)(copy.wait_send)

    @pl.when(jnp.logical_and(is_img, home))
    def _():
        for k in range(4):
            f_copy(k).wait_send()


def on_device(pooled, final_gain, head_weight, pair_ids, log_scale, bias):
    n, d = pooled.shape[1:]
    hbm = pl.BlockSpec(memory_space=pl.ANY)
    smem = pl.BlockSpec(memory_space=pltpu.SMEM)
    buf = lambda r, kind=BF: pltpu.VMEM((r, d), kind)
    dma = pltpu.SemaphoreType.DMA
    return pl.pallas_call(
        kernel,
        out_shape=pltpu.VMEM((1, n, d), F32),
        in_specs=[hbm, hbm, hbm, hbm, smem, smem],
        out_specs=pl.BlockSpec(memory_space=pltpu.VMEM),
        scratch_shapes=[
            buf(n), buf(1, F32), pltpu.VMEM((128, 128), jnp.int32), buf(d), buf(128), buf(1024), buf(1024), pltpu.VMEM((1024, 1024), BF), buf(1024, F32), buf(1024, F32),
            buf(1024), buf(256), buf(1024), buf(1024), buf(14 * 64), buf(4 * 64), buf(8 * 64), buf(6 * 64), buf(128),
            pltpu.VMEM((1024, 128), jnp.int32), pltpu.VMEM((8, 1024), jnp.int32),
            dma((4,)), dma((3, 2)), dma((2, 2)), dma((2, 2)), dma((2, 2)), dma((4,)), dma((4,)), dma((2, 6)), dma((2, 6)), dma((2, 14)), dma((2, 14)),
            dma((16,)), dma((16,)), dma((3,)), dma((3,)), dma((2, 14)), dma((2, 14)), dma((2, 12)), dma((2, 12)),
            dma((2, 4)), dma((3, 4)), dma((4,)), dma((4,)),
        ],
        compiler_params=pltpu.CompilerParams(collective_id=0, has_side_effects=True, vmem_limit_bytes=67043328 - 600000),
        name="towers",
    )(pooled, final_gain, head_weight, pair_ids.reshape(128, 128), log_scale, bias)


def solution(mesh):
    placed = (P("tower", "blk", None), P("tower", None), P("tower", None, None), P(), P(), P())
    return jax.shard_map(
        on_device, mesh=mesh, in_specs=placed, out_specs=P("tower", "blk", None), check_vma=False
    )
```
